256 devices in a mesh: dp: 64 (over y, z, x_lo), fsdp: 4 (over x_hi, core).
Axes of the slice: x: 4 (x_hi: 2, x_lo: 2; x = x_hi * 2 + x_lo), y: 4, z: 8, core: 2. Of those that a mesh axis runs over, the one named last changes fastest.
Arguments:
- picture_tower_inputs: bfloat16 [131072, 1152], P(('dp', 'fsdp')), may hold values from -6 to 6
- caption_tower_inputs: bfloat16 [131072, 1152], P(('dp', 'fsdp')), may hold values from -6 to 6
- halfwidth_parameter_matrix: bfloat16 [1152, 2304], P('fsdp'), may hold values from -0.1875 to 0.1875
- affinity_multiplier: float32 [1], replicated, may hold values from 4 to 12
- affinity_offset: float32 [1], replicated, may hold values from -6 to -2
- precise_parameter_copy: float32 [1152, 2304], P('fsdp', 'dp'), may hold values from -0.125 to 0.125
- gradient_mean_estimate: float32 [1152, 2304], P('fsdp', 'dp'), may hold values from -4 to 4
- gradient_variance_estimate: float32 [1152, 2304], P('fsdp', 'dp'), may hold values from 0.05 to 1
Outputs:
- img_tangent: bfloat16 [131072, 1152], P(('dp', 'fsdp'))
- txt_tangent: bfloat16 [131072, 1152], P(('dp', 'fsdp'))
- new_master: float32 [1152, 2304], P('fsdp', 'dp')
- new_one: float32 [1152, 2304], P('fsdp', 'dp')
- new_two: float32 [1152, 2304], P('fsdp', 'dp')
- new_weights: bfloat16 [1152, 2304], P('fsdp')
The draws below stay inside these ranges and needn't reach their ends.
All inputs are finite; a program needn't handle non-finite values.
Results may differ from the reference program's by a relative error of at most 0.008.
Values may be sent and summed in bfloat16 or wider, within the bound.
No kernel may reach another device: no remote copies, remote signals or barrier semaphores. Data moves between devices by JAX's collectives and lax.ppermute only.
A program may use at most 128 MiB of HBM per device.

```python
import math
import jax
import jax.numpy as jnp
from jax import lax

D = 1152
B_DEV = 512
CYCLE = 4
TOKENS = 131072
N_DP = 64
N_FSDP = 4


def level_of(rng, shape, pieces, smallest, high):
    factor_of, own = 1.0, jax.random.fold_in(rng, 6)
    for position, blocks in pieces:
        steps = jnp.exp(jax.random.uniform(jax.random.fold_in(own, position), (blocks,), jnp.float32, smallest / len(pieces), high / len(pieces)))
        factor_of = factor_of * jnp.repeat(steps, shape[position] // blocks).reshape([-1 if axis == position else 1 for axis in range(len(shape))])
    return factor_of


def bell_draw(own_key, shape, width, most, shards=(), held_as=jnp.bfloat16):
    factor_of = level_of(own_key, shape, shards, -0.22, 0.18) if shards else 1.0
    entries = jax.random.normal(own_key, shape, jnp.float32) * width * factor_of
    return jnp.minimum(jnp.maximum(entries, -most), most).astype(held_as)


def setup_inputs(seed: int = 0) -> dict:
    seeds = jax.random.split(jax.random.key(seed), 9)
    return {
        "picture_tower_inputs": bell_draw(seeds[0], (TOKENS, D), 1.0, 6.0, ((0, 256),)),
        "caption_tower_inputs": bell_draw(seeds[1], (TOKENS, D), 1.0, 6.0, ((0, 256),)),
        "halfwidth_parameter_matrix": bell_draw(seeds[2], (D, 2 * D), D ** -0.5, 0.1875, ((0, 4),)),
        "affinity_multiplier": jnp.clip(jnp.exp(jax.random.uniform(seeds[3], (1,), jnp.float32, math.log(4.0), math.log(12.0))), 4.0, 12.0),
        "affinity_offset": jnp.clip(jax.random.uniform(seeds[4], (1,), jnp.float32, -6.0, -2.0), -6.0, -2.0),
        "precise_parameter_copy": bell_draw(seeds[5], (D, 2 * D), 0.008, 0.125, ((0, 4), (1, 64)), jnp.float32),
        "gradient_mean_estimate": bell_draw(seeds[6], (D, 2 * D), 0.3, 4.0, ((0, 4), (1, 64)), jnp.float32),
        "gradient_variance_estimate": jnp.clip(jnp.exp(math.log(1.0) - 2.9957323 * jax.random.uniform(seeds[7], (D, 2 * D), jnp.float32) ** level_of(seeds[7], (D, 2 * D), ((0, 4), (1, 64)), -0.2, 0.2)), 0.05, 1.0),
    }


def normalize(projected):
    inv_norm = lax.rsqrt(lax.optimization_barrier(jnp.sum(projected * projected, axis=-1, keepdims=True)) + 1e-06)
    return (projected * inv_norm, inv_norm)

def reference(picture_tower_inputs, caption_tower_inputs, halfwidth_parameter_matrix, affinity_multiplier, affinity_offset, precise_parameter_copy, gradient_mean_estimate, gradient_variance_estimate):
    proj_img = jnp.dot(picture_tower_inputs, halfwidth_parameter_matrix[:, :D], preferred_element_type=jnp.float32)
    proj_txt = jnp.dot(caption_tower_inputs, halfwidth_parameter_matrix[:, D:], preferred_element_type=jnp.float32)
    unit_img, norm_img = normalize(proj_img)
    normalized_text, norm_txt = normalize(proj_txt)
    low_img = lax.optimization_barrier(unit_img.astype(jnp.bfloat16)).astype(jnp.float32)
    low_txt = lax.optimization_barrier(normalized_text.astype(jnp.bfloat16)).astype(jnp.float32)
    blocks_img = low_img.reshape(N_DP, N_FSDP, B_DEV, D)
    blocks_txt = low_txt.reshape(N_DP, N_FSDP, B_DEV, D)
    affinity_multiplier_name = affinity_multiplier[0]
    shift_value = affinity_offset[0]
    identity_mask = jnp.eye(B_DEV, dtype=jnp.float32)
    grad_img = jnp.zeros_like(blocks_img)
    grad_txt = jnp.zeros_like(blocks_txt)
    for cycle_step in range(CYCLE):
        visiting = jnp.roll(blocks_txt, cycle_step, axis=0)
        logits = affinity_multiplier_name * jnp.einsum('pfid,pfjd->pfij', blocks_img, visiting) + shift_value
        if cycle_step == 0:
            sign_label = 2.0 * identity_mask - 1.0
        else:
            sign_label = -jnp.ones_like(identity_mask)
        pair_weight = (-sign_label * jax.nn.sigmoid(-sign_label * logits) * affinity_multiplier_name).astype(jnp.bfloat16)
        pair_weight = lax.optimization_barrier(pair_weight).astype(jnp.float32)
        grad_img = grad_img + jnp.einsum('pfij,pfjd->pfid', pair_weight, visiting)
        grad_txt = grad_txt + jnp.roll(jnp.einsum('pfij,pfid->pfjd', pair_weight, blocks_img), -cycle_step, axis=0)
    grad_img = grad_img.reshape(TOKENS, D)
    grad_txt = grad_txt.reshape(TOKENS, D)
    img_tangent = (norm_img * (grad_img - unit_img * lax.optimization_barrier(jnp.sum(unit_img * grad_img, axis=1, keepdims=True)))).astype(jnp.bfloat16)
    txt_tangent = (norm_txt * (grad_txt - normalized_text * lax.optimization_barrier(jnp.sum(normalized_text * grad_txt, axis=1, keepdims=True)))).astype(jnp.bfloat16)
    gradient = jnp.concatenate([jnp.dot(picture_tower_inputs.T, img_tangent, preferred_element_type=jnp.float32), jnp.dot(caption_tower_inputs.T, txt_tangent, preferred_element_type=jnp.float32)], axis=1)
    new_one = 0.9 * gradient_mean_estimate + 0.1 * gradient
    new_two = 0.95 * gradient_variance_estimate + 0.05 * gradient * gradient
    new_master = precise_parameter_copy - 0.001 * (new_one / (jnp.sqrt(new_two) + 1e-08) + 0.1 * precise_parameter_copy)
    return (img_tangent, txt_tangent, new_master, new_one, new_two, new_master.astype(jnp.bfloat16))
```

```python
import jax
import jax.numpy as jnp
from jax import lax
from jax.sharding import Mesh, PartitionSpec as P

CYCLE = 4
PIECES = 2
LINE = ("y", "z")
AXES = ("y", "z", "xl", "xh", "c")
DP = ("y", "z", "xl")
FSDP = ("xh", "c")


def shifted(value, steps):
    count = lax.axis_size(LINE)
    return lax.ppermute(value, LINE, [(i, (i + steps) % count) for i in range(count)])


def swapped(value, axes):
    count = lax.axis_size(axes)
    return lax.ppermute(value, axes, [(i, count - 1 - i) for i in range(count)])


def normalize(projected):
    inv_norm = lax.rsqrt(jnp.sum(projected * projected, axis=-1, keepdims=True) + 1e-06)
    return (projected * inv_norm, inv_norm)


def rows_by_rows(left, right):
    return lax.dot_general(
        left, right, (((1,), (1,)), ((), ())), preferred_element_type=jnp.float32
    )


def contract_rows(left, right):
    return lax.dot_general(
        left, right, (((0,), (0,)), ((), ())), preferred_element_type=jnp.float32
    )


def gather_weights(own):
    rows = own.shape[0]
    across = swapped(own, ("xl", "xh"))
    beside = swapped(own, "c")
    far = swapped(across, "c")
    xh, c = lax.axis_index("xh"), lax.axis_index("c")
    full = jnp.zeros((4 * rows, own.shape[1]), own.dtype)
    for part, hi, lo in (
        (own, xh, c),
        (beside, xh, 1 - c),
        (across, 1 - xh, c),
        (far, 1 - xh, 1 - c),
    ):
        full = lax.dynamic_update_slice(full, part, ((hi * 2 + lo) * rows, 0))
    return full


def exchange(img, txt):
    even = lax.axis_index("xl") == 0
    two_t, two_i = shifted(txt, 1), shifted(img, -1)
    first = swapped(jnp.where(even, txt, img), "xl")
    second = swapped(jnp.where(even, two_i, two_t), "xl")
    one_t = jnp.where(even, second, first)
    one_i = jnp.where(even, first, second)
    three_t, three_i = shifted(one_t, 1), shifted(one_i, -1)
    return (one_t, two_t, three_t), (one_i, two_i, three_i)


def body(
    picture_tower_inputs,
    caption_tower_inputs,
    halfwidth_parameter_matrix,
    affinity_multiplier,
    affinity_offset,
    precise_parameter_copy,
    gradient_mean_estimate,
    gradient_variance_estimate,
):
    row_count, width = picture_tower_inputs.shape
    mult, offset = affinity_multiplier[0], affinity_offset[0]
    weights = gather_weights(halfwidth_parameter_matrix)
    w_img, w_txt = weights[:, :width], weights[:, width:]

    piece = row_count // PIECES
    texts, images = [], []
    for n in range(PIECES):
        cut = slice(n * piece, (n + 1) * piece)
        t, i = exchange(picture_tower_inputs[cut], caption_tower_inputs[cut])
        texts.append(t)
        images.append(i)

    def project(rows, w):
        return normalize(jnp.dot(rows, w, preferred_element_type=jnp.float32))

    unit_img, norm_img = project(picture_tower_inputs, w_img)
    unit_txt, norm_txt = project(caption_tower_inputs, w_txt)
    low_img, low_txt = unit_img.astype(jnp.bfloat16), unit_txt.astype(jnp.bfloat16)

    logits = mult * rows_by_rows(low_img, low_txt) + offset
    sign = 2.0 * jnp.eye(row_count, dtype=jnp.float32) - 1.0
    pair = (-sign * jax.nn.sigmoid(-sign * logits) * mult).astype(jnp.bfloat16)
    grad_img = jnp.dot(pair, low_txt, preferred_element_type=jnp.float32)
    grad_txt = contract_rows(pair, low_img)

    def against(mine, others):
        weight = (jax.nn.sigmoid(mult * rows_by_rows(mine, others) + offset) * mult).astype(
            jnp.bfloat16
        )
        return jnp.dot(weight, others, preferred_element_type=jnp.float32)

    for k in (1, 0, 2):
        for n in range(PIECES):
            other = project(texts[n][k], w_txt)[0].astype(jnp.bfloat16)
            grad_img = grad_img + against(low_img, other)
            other = project(images[n][k], w_img)[0].astype(jnp.bfloat16)
            grad_txt = grad_txt + against(low_txt, other)

    img_tangent = (
        norm_img * (grad_img - unit_img * jnp.sum(unit_img * grad_img, axis=1, keepdims=True))
    ).astype(jnp.bfloat16)
    txt_tangent = (
        norm_txt * (grad_txt - unit_txt * jnp.sum(unit_txt * grad_txt, axis=1, keepdims=True))
    ).astype(jnp.bfloat16)

    sides = jnp.concatenate(
        [
            contract_rows(img_tangent, picture_tower_inputs),
            contract_rows(txt_tangent, caption_tower_inputs),
        ],
        axis=0,
    )
    n_y, n_z = lax.axis_size("y"), lax.axis_size("z")
    share = width // 4
    cols = 2 * width // (n_y * n_z * 2)
    lanes = 128
    sides = sides.astype(jnp.bfloat16).reshape(n_y, n_z, 2, cols, 2, 2, share)
    sides = sides.transpose(5, 0, 2, 4, 1, 3, 6).reshape(
        2, n_y * 4, n_z * cols * share // lanes, lanes
    )
    c = lax.axis_index("c")
    give = lax.dynamic_index_in_dim(sides, 1 - c, 0, keepdims=False)
    keep = lax.dynamic_index_in_dim(sides, c, 0, keepdims=False)
    got = swapped(give, "c")
    chip = (keep.astype(jnp.float32) + got.astype(jnp.float32)).astype(jnp.bfloat16)
    parts = lax.all_to_all(chip, ("y", "xl", "xh"), 0, 0, tiled=True)
    plane = jnp.sum(parts.astype(jnp.float32), axis=0).astype(jnp.bfloat16)
    plane = plane.reshape(n_z, cols * share // lanes, lanes)
    parts = lax.all_to_all(plane, "z", 0, 0, tiled=True)
    gradient = jnp.sum(parts.astype(jnp.float32), axis=0).reshape(cols, share).T

    new_one = 0.9 * gradient_mean_estimate + 0.1 * gradient
    new_two = 0.95 * gradient_variance_estimate + 0.05 * gradient * gradient
    new_master = precise_parameter_copy - 0.001 * (
        new_one / (jnp.sqrt(new_two) + 1e-08) + 0.1 * precise_parameter_copy
    )
    mine = new_master.astype(jnp.bfloat16).T.reshape(1, cols * share // lanes, lanes)
    line = lax.all_to_all(
        jnp.broadcast_to(mine, (n_z,) + mine.shape[1:]), "z", 0, 0, tiled=True
    )
    line = line.reshape(1, n_z * cols * share // lanes, lanes)
    all_cols = lax.all_to_all(
        jnp.broadcast_to(line, (n_y * 2,) + line.shape[1:]), ("y", "xl"), 0, 0, tiled=True
    )
    new_weights = (
        all_cols.reshape(n_y, 2, n_z, cols, share)
        .transpose(4, 0, 2, 1, 3)
        .reshape(share, n_y * n_z * 2 * cols)
    )
    return (img_tangent, txt_tangent, new_master, new_one, new_two, new_weights)


def solution(mesh):
    fine = Mesh(mesh.devices.reshape(4, 8, 2, 2, 2), AXES)
    rows = P(DP + FSDP, None)
    state = P(FSDP, DP)
    return jax.shard_map(
        body,
        mesh=fine,
        in_specs=(rows, rows, P(FSDP, None), P(), P(), state, state, state),
        out_specs=(rows, rows, state, state, state, P(FSDP, None)),
        check_vma=False,
    )
```

```python
import jax
import jax.numpy as jnp
from jax import lax
from jax.experimental import pallas as pl
from jax.experimental.pallas import tpu as pltpu
from jax.sharding import Mesh, PartitionSpec as P

CYCLE = 4
PIECES = 2
LINE = ("y", "z")
AXES = ("y", "z", "xl", "xh", "c")
DP = ("y", "z", "xl")
FSDP = ("xh", "c")


def shifted(value, steps):
    count = lax.axis_size(LINE)
    return lax.ppermute(value, LINE, [(i, (i + steps) % count) for i in range(count)])


def swapped(value, axes):
    count = lax.axis_size(axes)
    return lax.ppermute(value, axes, [(i, count - 1 - i) for i in range(count)])


def gather_weights(own):
    rows = own.shape[0]
    across = swapped(own, ("xl", "xh"))
    beside = swapped(own, "c")
    far = swapped(across, "c")
    xh, c = lax.axis_index("xh"), lax.axis_index("c")
    full = jnp.zeros((4 * rows, own.shape[1]), own.dtype)
    for part, hi, lo in (
        (own, xh, c),
        (beside, xh, 1 - c),
        (across, 1 - xh, c),
        (far, 1 - xh, 1 - c),
    ):
        full = lax.dynamic_update_slice(full, part, ((hi * 2 + lo) * rows, 0))
    return full


def exchange(img, txt):
    even = lax.axis_index("xl") == 0
    two_t, two_i = shifted(txt, 1), shifted(img, -1)
    first = swapped(jnp.where(even, txt, img), "xl")
    second = swapped(jnp.where(even, two_i, two_t), "xl")
    one_t = jnp.where(even, second, first)
    one_i = jnp.where(even, first, second)
    three_t, three_i = shifted(one_t, 1), shifted(one_i, -1)
    return (one_t, two_t, three_t), (one_i, two_i, three_i)


WIDTH = 1152
ROWS = 512
SHARE = 288
COLS = 36
FOLD = 3
TALL = SHARE // FOLD
LANES = 896
TILE = 256
VMEM = pl.BlockSpec(memory_space=pltpu.VMEM)
SMEM = pl.BlockSpec(memory_space=pltpu.SMEM)


def dot(left, right, dims):
    return lax.dot_general(left, right, (dims, ((), ())), preferred_element_type=jnp.float32)


def project(rows, w):
    projected = dot(rows, w, ((1,), (0,)))
    norm = lax.rsqrt(jnp.sum(projected * projected, axis=-1, keepdims=True) + 1e-06)
    return projected * norm, norm


def own_kernel(mult_ref, offset_ref, img, txt, w, unit_i, unit_t, norm_i, norm_t, low_i, low_t, acc_i, acc_t):
    mult, offset = mult_ref[0], offset_ref[0]

    def step(n, carry):
        rows = pl.ds(pl.multiple_of(n * TILE, TILE), TILE)
        for raw, side, unit, norm, low in (
            (img, 0, unit_i, norm_i, low_i),
            (txt, 1, unit_t, norm_t, low_t),
        ):
            u, inv = project(raw[rows, :], w[:, side * WIDTH : (side + 1) * WIDTH])
            unit[rows, :] = u
            norm[rows, :] = inv
            low[rows, :] = u.astype(jnp.bfloat16)
        return carry

    lax.fori_loop(0, ROWS // TILE, step, 0)
    logits = mult * dot(low_i[...], low_t[...], ((1,), (1,))) + offset
    line = lax.broadcasted_iota(jnp.int32, logits.shape, 0)
    column = lax.broadcasted_iota(jnp.int32, logits.shape, 1)
    sign = jnp.where(line == column, 1.0, -1.0)
    pair = (-sign * jax.nn.sigmoid(-sign * logits) * mult).astype(jnp.bfloat16)
    acc_i[...] = dot(pair, low_t[...], ((1,), (0,)))
    acc_t[...] = dot(pair, low_i[...], ((0,), (0,)))


def meet_kernel(mult_ref, offset_ref, raw_t, raw_i, w, low_i, low_t, in_i, in_t, acc_i, acc_t):
    mult, offset = mult_ref[0], offset_ref[0]
    acc_i[...] = in_i[...]
    acc_t[...] = in_t[...]

    def step(n, carry):
        rows = pl.ds(pl.multiple_of(n * TILE, TILE), TILE)
        for raw, side, mine, acc in ((raw_t, 1, low_i, acc_i), (raw_i, 0, low_t, acc_t)):
            other = project(raw[rows, :], w[:, side * WIDTH : (side + 1) * WIDTH])[0]
            other = other.astype(jnp.bfloat16)
            logits = mult * dot(mine[...], other, ((1,), (1,))) + offset
            weight = (jax.nn.sigmoid(logits) * mult).astype(jnp.bfloat16)
            acc[...] += dot(weight, other, ((1,), (0,)))
        return carry

    lax.fori_loop(0, raw_t.shape[0] // TILE, step, 0)


def fill(chunks, tans, xs):
    for t in range(2):
        for xh in range(2):
            g = dot(tans[t][...], xs[t][xh], ((0,), (0,)))
            for block in range(4):
                top = block * SHARE
                pieces = [g[top + q * TALL : top + (q + 1) * TALL] for q in range(FOLD)]
                pieces.append(jnp.zeros((TALL, LANES - FOLD * SHARE), jnp.float32))
                chunks[(t * 4 + block) * 2 + xh] = jnp.concatenate(pieces, axis=1).astype(
                    jnp.bfloat16
                )


def tail_kernel(acc_i, acc_t, unit_i, unit_t, norm_i, norm_t, x_i, x_t, tan_i, tan_t, chunks):
    def step(n, carry):
        rows = pl.ds(pl.multiple_of(n * 64, 64), 64)
        for acc, unit, norm, tan in ((acc_i, unit_i, norm_i, tan_i), (acc_t, unit_t, norm_t, tan_t)):
            u, a = unit[rows, :], acc[rows, :]
            along = jnp.sum(u * a, axis=-1, keepdims=True)
            tan[rows, :] = (norm[rows, :] * (a - u * along)).astype(jnp.bfloat16)
        return carry

    lax.fori_loop(0, ROWS // 64, step, 0)
    fill(chunks, (tan_i, tan_t), (x_i, x_t))


def keep_kernel(tan_i, tan_t, x_i, x_t, chunks):
    fill(chunks, (tan_i, tan_t), (x_i, x_t))


def weave_kernel(parts, order, out):
    for half in range(2):
        total = jnp.zeros((SHARE, WIDTH), jnp.float32)
        stack = []
        for block in range(4):
            for q in range(FOLD):
                stack.append(parts[half * 4 + block, :, q * SHARE : (q + 1) * SHARE])
        total = dot(jnp.concatenate(stack, axis=0), order[...], ((0,), (0,)))
        out[:, half * WIDTH : (half + 1) * WIDTH] = total.astype(jnp.bfloat16)


def call(kernel, name, outs, args, flops, scalars=0, aliases=None):
    moved = sum(a.size * a.dtype.itemsize for a in (*args, *outs))
    return pl.pallas_call(
        kernel,
        name=name,
        out_shape=outs,
        in_specs=[SMEM] * scalars + [VMEM] * (len(args) - scalars),
        out_specs=[VMEM] * len(outs),
        input_output_aliases=aliases or {},
        cost_estimate=pl.CostEstimate(flops=flops, bytes_accessed=moved, transcendentals=0),
        compiler_params=pltpu.CompilerParams(vmem_limit_bytes=56 * 1024 * 1024),
    )(*args)


def shaped(shape, dtype):
    return jax.ShapeDtypeStruct(shape, dtype)


def column_order():
    p = lax.iota(jnp.int32, WIDTH)
    y, xl = p // 576, p % 576 // 288
    q, z, i = p % 288 // 96, p % 96 // 12, p % 12
    natural = ((y * 8 + z) * 2 + xl) * COLS + q * 12 + i
    return (natural[:, None] == lax.iota(jnp.int32, WIDTH)[None, :]).astype(jnp.bfloat16)


def body(
    picture_tower_inputs,
    caption_tower_inputs,
    halfwidth_parameter_matrix,
    affinity_multiplier,
    affinity_offset,
    precise_parameter_copy,
    gradient_mean_estimate,
    gradient_variance_estimate,
):
    bf16, f32 = jnp.bfloat16, jnp.float32
    img, txt = picture_tower_inputs, caption_tower_inputs
    scalars = (affinity_multiplier, affinity_offset)
    order = column_order()
    w = halfwidth_parameter_matrix
    w = jnp.concatenate(
        [
            dot(w[:, :WIDTH], order, ((1,), (1,))).astype(bf16),
            dot(w[:, WIDTH:], order, ((1,), (1,))).astype(bf16),
        ],
        axis=1,
    )
    weights = gather_weights(w)

    piece = ROWS // PIECES
    texts, images = [], []
    for n in range(PIECES):
        cut = slice(n * piece, (n + 1) * piece)
        t, i = exchange(img[cut], txt[cut])
        texts.append(t)
        images.append(i)

    c = lax.axis_index("c")

    def columns(rows, core):
        parts = rows.reshape(ROWS, 2, 2, SHARE)
        return jnp.where(core == 0, parts[:, :, 0], parts[:, :, 1]).transpose(1, 0, 2)

    give_i, give_t = columns(img, 1 - c), columns(txt, 1 - c)
    keep_i, keep_t = columns(img, c), columns(txt, c)

    big, flat = shaped((ROWS, WIDTH), f32), shaped((ROWS, 1), f32)
    low = shaped((ROWS, WIDTH), bf16)
    mac = 2 * ROWS * WIDTH
    unit_i, unit_t, norm_i, norm_t, low_i, low_t, acc_i, acc_t = call(
        own_kernel,
        "own",
        (big, big, flat, flat, low, low, big, big),
        (*scalars, img, txt, weights),
        mac * (2 * WIDTH + 3 * ROWS),
        scalars=2,
    )
    for k in (1, 0, 2):
        for n in range(PIECES):
            acc_i, acc_t = call(
                meet_kernel,
                "meet",
                (big, big),
                (*scalars, texts[n][k], images[n][k], weights, low_i, low_t, acc_i, acc_t),
                mac * (2 * WIDTH + 4 * ROWS) // PIECES,
                scalars=2,
                aliases={7: 0, 8: 1},
            )

    chunk = shaped((16, TALL, LANES), bf16)
    tan_i, tan_t, give = call(
        tail_kernel,
        "tail",
        (low, low, chunk),
        (acc_i, acc_t, unit_i, unit_t, norm_i, norm_t, give_i, give_t),
        mac * WIDTH,
    )
    got = swapped(give, "c")
    (keep,) = call(keep_kernel, "keep", (chunk,), (tan_i, tan_t, keep_i, keep_t), mac * WIDTH)
    img_tangent = dot(tan_i, order, ((1,), (0,))).astype(bf16)
    txt_tangent = dot(tan_t, order, ((1,), (0,))).astype(bf16)

    chip = (keep.astype(f32) + got.astype(f32)).astype(bf16)
    parts = lax.all_to_all(chip, ("y", "xl", "xh"), 0, 0, tiled=True)
    plane = jnp.sum(parts.astype(f32), axis=0).astype(bf16)
    parts = lax.all_to_all(plane.reshape(8, 12, LANES), "z", 0, 0, tiled=True)
    gradient = jnp.sum(parts.astype(f32), axis=0)[:, : FOLD * SHARE]
    gradient = gradient.reshape(12, FOLD, SHARE).transpose(2, 1, 0).reshape(SHARE, COLS)

    new_one = 0.9 * gradient_mean_estimate + 0.1 * gradient
    new_two = 0.95 * gradient_variance_estimate + 0.05 * gradient * gradient
    new_master = precise_parameter_copy - 0.001 * (
        new_one / (jnp.sqrt(new_two) + 1e-08) + 0.1 * precise_parameter_copy
    )
    mine = new_master.astype(bf16).reshape(SHARE, FOLD, 12).transpose(2, 1, 0)
    mine = jnp.pad(mine.reshape(1, 12, FOLD * SHARE), ((0, 0), (0, 0), (0, LANES - FOLD * SHARE)))
    line = lax.all_to_all(jnp.broadcast_to(mine, (8, 12, LANES)), "z", 0, 0, tiled=True)
    line = jnp.broadcast_to(line.reshape(1, TALL, LANES), (8, TALL, LANES))
    parts = lax.all_to_all(line, ("y", "xl"), 0, 0, tiled=True)
    (new_weights,) = call(
        weave_kernel,
        "weave",
        (shaped((SHARE, 2 * WIDTH), bf16),),
        (parts, order),
        4 * SHARE * WIDTH * WIDTH,
    )
    return (img_tangent, txt_tangent, new_master, new_one, new_two, new_weights)


def solution(mesh):
    fine = Mesh(mesh.devices.reshape(4, 8, 2, 2, 2), AXES)
    rows = P(DP + FSDP, None)
    state = P(FSDP, DP)
    return jax.shard_map(
        body,
        mesh=fine,
        in_specs=(rows, rows, P(FSDP, None), P(), P(), state, state, state),
        out_specs=(rows, rows, state, state, state, P(FSDP, None)),
        check_vma=False,
    )
```

```python
import jax
import jax.numpy as jnp
from jax import lax
from jax.experimental import pallas as pl
from jax.experimental.pallas import tpu as pltpu
from jax.sharding import Mesh, PartitionSpec as P

PIECES = 2
LINE = ("y", "z")
AXES = ("y", "z", "xl", "xh", "c")
DP = ("y", "z", "xl")
FSDP = ("xh", "c")


def shifted(value, steps):
    count = lax.axis_size(LINE)
    return lax.ppermute(value, LINE, [(i, (i + steps) % count) for i in range(count)])


def swapped(value, axes):
    count = lax.axis_size(axes)
    return lax.ppermute(value, axes, [(i, count - 1 - i) for i in range(count)])


def gather_weights(own):
    across = swapped(own, ("xl", "xh"))
    beside = swapped(own, "c")
    far = swapped(across, "c")
    xh, c = lax.axis_index("xh"), lax.axis_index("c")
    rows = own.shape[0]
    tops = jnp.stack([2 * xh + c, 2 * xh + 1 - c, 2 - 2 * xh + c, 3 - 2 * xh - c]) * rows
    return tops.astype(jnp.int32), (own, beside, across, far)


def exchange(img, txt):
    even = lax.axis_index("xl") == 0
    two_t = shifted(txt, 1)
    two_i = shifted(img, -1)
    first = swapped(jnp.where(even, txt, img), "xl")
    one_t, one_i, three_t, three_i = [], [], [], []
    piece = txt.shape[0] // PIECES
    seconds = []
    for n in range(PIECES):
        cut = slice(n * piece, (n + 1) * piece)
        held = jnp.where(even, two_i[cut], two_t[cut])
        seconds.append(swapped(held, "xl"))
    for n in range(PIECES):
        cut = slice(n * piece, (n + 1) * piece)
        one_t.append(jnp.where(even, seconds[n], first[cut]))
        one_i.append(jnp.where(even, first[cut], seconds[n]))
        three_t.append(shifted(one_t[n], 1))
        three_i.append(shifted(one_i[n], -1))
    return one_t, one_i, two_t, two_i, three_t, three_i


WIDTH = 1152
ROWS = 512
SHARE = 288
COLS = 36
FOLD = 3
TALL = SHARE // FOLD
LANES = 896
TILE = 256
VMEM = pl.BlockSpec(memory_space=pltpu.VMEM)
SMEM = pl.BlockSpec(memory_space=pltpu.SMEM)


def dot(left, right, dims):
    return lax.dot_general(left, right, (dims, ((), ())), preferred_element_type=jnp.float32)


def project(rows, w):
    projected = dot(rows, w, ((1,), (0,)))
    norm = lax.rsqrt(jnp.sum(projected * projected, axis=-1, keepdims=True) + 1e-06)
    return projected * norm, norm


class Loads:
    def __init__(self, sems):
        self.sems, self.used = sems, 0

    def start(self, source, target):
        copy = pltpu.make_async_copy(source, target, self.sems.at[self.used])
        self.used += 1
        copy.start()
        return copy


def load_weights(loads, tops, shards, w):
    copies = []
    for n, shard in enumerate(shards):
        top = pl.multiple_of(tops[n], 32)
        copies.append(loads.start(shard, w.at[pl.ds(top, SHARE), :]))
    return copies


def load_rows(loads, pieces, raw):
    rows = pieces[0].shape[0]
    return [loads.start(p, raw.at[pl.ds(n * rows, rows), :]) for n, p in enumerate(pieces)]


def wait(*groups):
    for group in groups:
        for copy in group:
            copy.wait()


def meet(raw, side, w, mine, acc, mult, offset):
    def step(n, carry):
        rows = pl.ds(pl.multiple_of(n * TILE, TILE), TILE)
        other = project(raw[rows, :], w[:, side * WIDTH : (side + 1) * WIDTH])[0]
        other = other.astype(jnp.bfloat16)
        logits = mult * dot(mine[...], other, ((1,), (1,))) + offset
        weight = (jax.nn.sigmoid(logits) * mult).astype(jnp.bfloat16)
        acc[...] += dot(weight, other, ((1,), (0,)))
        return carry

    lax.fori_loop(0, ROWS // TILE, step, 0)


def own_kernel(mult_ref, offset_ref, tops, *refs):
    shards, (img, txt, two_t, two_i), rest = refs[:4], refs[4:8], refs[8:]
    unit_i, unit_t, norm_i, norm_t, low_i, low_t, acc_i, acc_t = rest[:8]
    w, own_i, own_t, raw_t, raw_i, sems = rest[8:]
    mult, offset = mult_ref[0], offset_ref[0]
    loads = Loads(sems)
    first = load_weights(loads, tops, shards, w)
    first += load_rows(loads, [img], own_i) + load_rows(loads, [txt], own_t)
    later = load_rows(loads, [two_t], raw_t) + load_rows(loads, [two_i], raw_i)
    wait(first)

    def step(n, carry):
        rows = pl.ds(pl.multiple_of(n * TILE, TILE), TILE)
        for raw, side, unit, norm, low in (
            (own_i, 0, unit_i, norm_i, low_i),
            (own_t, 1, unit_t, norm_t, low_t),
        ):
            u, inv = project(raw[rows, :], w[:, side * WIDTH : (side + 1) * WIDTH])
            unit[rows, :] = u
            norm[rows, :] = inv
            low[rows, :] = u.astype(jnp.bfloat16)
        return carry

    lax.fori_loop(0, ROWS // TILE, step, 0)
    logits = mult * dot(low_i[...], low_t[...], ((1,), (1,))) + offset
    line = lax.broadcasted_iota(jnp.int32, logits.shape, 0)
    column = lax.broadcasted_iota(jnp.int32, logits.shape, 1)
    sign = jnp.where(line == column, 1.0, -1.0)
    pair = (-sign * jax.nn.sigmoid(-sign * logits) * mult).astype(jnp.bfloat16)
    acc_i[...] = dot(pair, low_t[...], ((1,), (0,)))
    acc_t[...] = dot(pair, low_i[...], ((0,), (0,)))
    wait(later)
    meet(raw_t, 1, w, low_i, acc_i, mult, offset)
    meet(raw_i, 0, w, low_t, acc_t, mult, offset)


def meet_kernel(mult_ref, offset_ref, tops, *refs):
    shards, refs = refs[:4], refs[4:]
    texts, images, refs = refs[:PIECES], refs[PIECES : 2 * PIECES], refs[2 * PIECES :]
    in_low_i, in_low_t, in_i, in_t, acc_i, acc_t, w, raw_t, raw_i, low_i, low_t, sems = refs
    mult, offset = mult_ref[0], offset_ref[0]
    loads = Loads(sems)
    first = load_weights(loads, tops, shards, w) + load_rows(loads, texts, raw_t)
    first += load_rows(loads, [in_low_i], low_i) + load_rows(loads, [in_i], acc_i)
    later = load_rows(loads, images, raw_i)
    later += load_rows(loads, [in_low_t], low_t) + load_rows(loads, [in_t], acc_t)
    wait(first)
    meet(raw_t, 1, w, low_i, acc_i, mult, offset)
    wait(later)
    meet(raw_i, 0, w, low_t, acc_t, mult, offset)


def tail_kernel(mult_ref, offset_ref, tops, *refs):
    shards, refs = refs[:4], refs[4:]
    texts, images, refs = refs[:PIECES], refs[PIECES : 2 * PIECES], refs[2 * PIECES :]
    in_low_i, in_low_t, in_i, in_t, in_unit_i, in_unit_t, in_norm_i, in_norm_t, in_x_i, in_x_t = refs[:10]
    tan_i, tan_t, chunks, w, raw_t, raw_i, low_i, low_t, acc_i, acc_t = refs[10:20]
    unit_i, unit_t, norm_i, norm_t, x_i, x_t, sems = refs[20:]
    mult, offset = mult_ref[0], offset_ref[0]
    loads = Loads(sems)
    first = load_weights(loads, tops, shards, w) + load_rows(loads, texts, raw_t)
    first += load_rows(loads, [in_low_i], low_i) + load_rows(loads, [in_i], acc_i)
    later = load_rows(loads, images, raw_i)
    later += load_rows(loads, [in_low_t], low_t) + load_rows(loads, [in_t], acc_t)
    wait(first)
    last = []
    for source, target in (
        (in_unit_i, unit_i),
        (in_unit_t, unit_t),
        (in_norm_i, norm_i),
        (in_norm_t, norm_t),
        (in_x_i, x_i),
        (in_x_t, x_t),
    ):
        last.append(loads.start(source, target))
    meet(raw_t, 1, w, low_i, acc_i, mult, offset)
    wait(later)
    meet(raw_i, 0, w, low_t, acc_t, mult, offset)
    wait(last)

    def step(n, carry):
        rows = pl.ds(pl.multiple_of(n * 64, 64), 64)
        for acc, unit, norm, tan in ((acc_i, unit_i, norm_i, tan_i), (acc_t, unit_t, norm_t, tan_t)):
            u, a = unit[rows, :], acc[rows, :]
            along = jnp.sum(u * a, axis=-1, keepdims=True)
            tan[rows, :] = (norm[rows, :] * (a - u * along)).astype(jnp.bfloat16)
        return carry

    lax.fori_loop(0, ROWS // 64, step, 0)
    fill(chunks, (tan_i, tan_t), (x_i, x_t))


def fill(chunks, tans, xs):
    for t in range(2):
        for xh in range(2):
            g = dot(tans[t][...], xs[t][xh], ((0,), (0,)))
            for block in range(4):
                top = block * SHARE
                pieces = [g[top + q * TALL : top + (q + 1) * TALL] for q in range(FOLD)]
                pieces.append(jnp.zeros((TALL, LANES - FOLD * SHARE), jnp.float32))
                chunks[(t * 4 + block) * 2 + xh] = jnp.concatenate(pieces, axis=1).astype(
                    jnp.bfloat16
                )


def keep_kernel(tan_i, tan_t, x_i, x_t, chunks):
    fill(chunks, (tan_i, tan_t), (x_i, x_t))


def weave_kernel(parts, order, out):
    for half in range(2):
        total = jnp.zeros((SHARE, WIDTH), jnp.float32)
        stack = []
        for block in range(4):
            for q in range(FOLD):
                stack.append(parts[half * 4 + block, :, q * SHARE : (q + 1) * SHARE])
        total = dot(jnp.concatenate(stack, axis=0), order[...], ((0,), (0,)))
        out[:, half * WIDTH : (half + 1) * WIDTH] = total.astype(jnp.bfloat16)


def call(kernel, outs, args, flops, scalars=0, scratch=(), anywhere=False):
    moved = sum(a.size * a.dtype.itemsize for a in (*args, *outs))
    spec = pl.BlockSpec(memory_space=pl.ANY) if anywhere else VMEM
    copies = (pltpu.SemaphoreType.DMA((len(args) - scalars,)),) if anywhere else ()
    return pl.pallas_call(
        kernel,
        out_shape=outs,
        in_specs=[SMEM] * scalars + [spec] * (len(args) - scalars),
        out_specs=[VMEM] * len(outs),
        scratch_shapes=(*scratch, *copies),
        cost_estimate=pl.CostEstimate(flops=flops, bytes_accessed=moved, transcendentals=0),
        compiler_params=pltpu.CompilerParams(vmem_limit_bytes=56 * 1024 * 1024),
    )(*args)


def shaped(shape, dtype):
    return jax.ShapeDtypeStruct(shape, dtype)


def column_order():
    p = lax.iota(jnp.int32, WIDTH)
    y, xl = p // 576, p % 576 // 288
    q, z, i = p % 288 // 96, p % 96 // 12, p % 12
    natural = ((y * 8 + z) * 2 + xl) * COLS + q * 12 + i
    return (natural[:, None] == lax.iota(jnp.int32, WIDTH)[None, :]).astype(jnp.bfloat16)


def inner(
    picture_tower_inputs,
    caption_tower_inputs,
    halfwidth_parameter_matrix,
    affinity_multiplier,
    affinity_offset,
    precise_parameter_copy,
    gradient_mean_estimate,
    gradient_variance_estimate,
):
    bf16, f32 = jnp.bfloat16, jnp.float32
    img, txt = picture_tower_inputs, caption_tower_inputs
    order = column_order()
    w = halfwidth_parameter_matrix
    w = jnp.concatenate(
        [
            dot(w[:, :WIDTH], order, ((1,), (1,))).astype(bf16),
            dot(w[:, WIDTH:], order, ((1,), (1,))).astype(bf16),
        ],
        axis=1,
    )
    tops, shards = gather_weights(w)
    scalars = (affinity_multiplier, affinity_offset, tops)

    one_t, one_i, two_t, two_i, three_t, three_i = exchange(img, txt)
    c = lax.axis_index("c")

    def columns(rows, core):
        parts = rows.reshape(ROWS, 2, 2, SHARE)
        return jnp.where(core == 0, parts[:, :, 0], parts[:, :, 1]).transpose(1, 0, 2)

    give_i, give_t = columns(img, 1 - c), columns(txt, 1 - c)
    keep_i, keep_t = columns(img, c), columns(txt, c)

    big, flat = shaped((ROWS, WIDTH), f32), shaped((ROWS, 1), f32)
    low = shaped((ROWS, WIDTH), bf16)
    mac = 2 * ROWS * WIDTH
    vw, vlow, vbig = pltpu.VMEM((WIDTH, 2 * WIDTH), bf16), pltpu.VMEM((ROWS, WIDTH), bf16), pltpu.VMEM((ROWS, WIDTH), f32)
    vflat, vx = pltpu.VMEM((ROWS, 1), f32), pltpu.VMEM((2, ROWS, SHARE), bf16)
    unit_i, unit_t, norm_i, norm_t, low_i, low_t, acc_i, acc_t = call(
        own_kernel,
        (big, big, flat, flat, low, low, big, big),
        (*scalars, *shards, img, txt, two_t, two_i),
        mac * (4 * WIDTH + 7 * ROWS),
        scalars=3,
        scratch=(vw, vlow, vlow, vlow, vlow),
        anywhere=True,
    )
    acc_i, acc_t = call(
        meet_kernel,
        (big, big),
        (*scalars, *shards, *one_t, *one_i, low_i, low_t, acc_i, acc_t),
        mac * (2 * WIDTH + 4 * ROWS),
        scalars=3,
        scratch=(vw, vlow, vlow, vlow, vlow),
        anywhere=True,
    )
    chunk = shaped((16, TALL, LANES), bf16)
    tan_i, tan_t, give = call(
        tail_kernel,
        (low, low, chunk),
        (
            *(*scalars, *shards, *three_t, *three_i, low_i, low_t, acc_i, acc_t),
            *(unit_i, unit_t, norm_i, norm_t, give_i, give_t),
        ),
        mac * (3 * WIDTH + 4 * ROWS),
        scalars=3,
        scratch=(vw, *(vlow,) * 4, *(vbig,) * 4, vflat, vflat, vx, vx),
        anywhere=True,
    )
    got = swapped(give, "c")
    (keep,) = call(keep_kernel, (chunk,), (tan_i, tan_t, keep_i, keep_t), mac * WIDTH)
    img_tangent = dot(tan_i, order, ((1,), (0,))).astype(bf16)
    txt_tangent = dot(tan_t, order, ((1,), (0,))).astype(bf16)

    chip = (keep.astype(f32) + got.astype(f32)).astype(bf16)
    parts = lax.all_to_all(chip, ("y", "xl", "xh"), 0, 0, tiled=True)
    plane = jnp.sum(parts.astype(f32), axis=0).astype(bf16)
    parts = lax.all_to_all(plane.reshape(8, 12, LANES), "z", 0, 0, tiled=True)
    gradient = jnp.sum(parts.astype(f32), axis=0)[:, : FOLD * SHARE]
    gradient = gradient.reshape(12, FOLD, SHARE).transpose(2, 1, 0).reshape(SHARE, COLS)

    new_one = 0.9 * gradient_mean_estimate + 0.1 * gradient
    new_two = 0.95 * gradient_variance_estimate + 0.05 * gradient * gradient
    new_master = precise_parameter_copy - 0.001 * (
        new_one / (jnp.sqrt(new_two) + 1e-08) + 0.1 * precise_parameter_copy
    )
    mine = new_master.astype(bf16).reshape(SHARE, FOLD, 12).transpose(2, 1, 0)
    mine = jnp.pad(mine.reshape(1, 12, FOLD * SHARE), ((0, 0), (0, 0), (0, LANES - FOLD * SHARE)))
    line = lax.all_to_all(jnp.broadcast_to(mine, (8, 12, LANES)), "z", 0, 0, tiled=True)
    line = jnp.broadcast_to(line.reshape(1, TALL, LANES), (8, TALL, LANES))
    parts = lax.all_to_all(line, ("y", "xl"), 0, 0, tiled=True)
    (new_weights,) = call(
        weave_kernel, (shaped((SHARE, 2 * WIDTH), bf16),), (parts, order), 4 * SHARE * WIDTH * WIDTH
    )
    return (img_tangent, txt_tangent, new_master, new_one, new_two, new_weights)


def solution(mesh):
    fine = Mesh(mesh.devices.reshape(4, 8, 2, 2, 2), AXES)
    rows = P(DP + FSDP, None)
    state = P(FSDP, DP)
    return jax.shard_map(
        inner,
        mesh=fine,
        in_specs=(rows, rows, P(FSDP, None), P(), P(), state, state, state),
        out_specs=(rows, rows, state, state, state, P(FSDP, None)),
        check_vma=False,
    )
```

```python
import functools

import jax
import jax.numpy as jnp
from jax import lax
from jax.experimental import pallas as pl
from jax.experimental.pallas import tpu as pltpu
from jax.sharding import Mesh, PartitionSpec as P

PIECES = 2
LINE = ("y", "z")
AXES = ("y", "z", "xl", "xh", "c")
DP = ("y", "z", "xl")
FSDP = ("xh", "c")


def shifted(value, steps):
    count = lax.axis_size(LINE)
    return lax.ppermute(value, LINE, [(i, (i + steps) % count) for i in range(count)])


def swapped(value, axes):
    count = lax.axis_size(axes)
    return lax.ppermute(value, axes, [(i, count - 1 - i) for i in range(count)])


def gather_weights(own):
    across = swapped(own, ("xl", "xh"))
    beside = swapped(own, "c")
    far = swapped(across, "c")
    xh, c = lax.axis_index("xh"), lax.axis_index("c")
    rows = own.shape[0]
    tops = jnp.stack([2 * xh + c, 2 * xh + 1 - c, 2 - 2 * xh + c, 3 - 2 * xh - c]) * rows
    return tops.astype(jnp.int32), (own, beside, across, far)


def exchange(img, txt):
    even = lax.axis_index("xl") == 0
    two_t = shifted(txt, 1)
    two_i = shifted(img, -1)
    first = swapped(jnp.where(even, txt, img), "xl")
    one_t, one_i, three_t, three_i = [], [], [], []
    piece = txt.shape[0] // PIECES
    seconds = []
    for n in range(PIECES):
        cut = slice(n * piece, (n + 1) * piece)
        held = jnp.where(even, two_i[cut], two_t[cut])
        seconds.append(swapped(held, "xl"))
    for n in range(PIECES):
        cut = slice(n * piece, (n + 1) * piece)
        near, far = lax.optimization_barrier((first, seconds[n]))
        one_t.append(jnp.where(even, far, near[cut]))
        one_i.append(jnp.where(even, near[cut], far))
        three_t.append(shifted(one_t[n], 1))
        three_i.append(shifted(one_i[n], -1))
    return one_t, one_i, two_t, two_i, three_t, three_i


WIDTH = 1152
ROWS = 512
SHARE = 288
COLS = 36
FOLD = 3
TALL = SHARE // FOLD
LANES = 896
VMEM = pl.BlockSpec(memory_space=pltpu.VMEM)
SMEM = pl.BlockSpec(memory_space=pltpu.SMEM)


def dot(left, right, dims):
    return lax.dot_general(left, right, (dims, ((), ())), preferred_element_type=jnp.float32)


def project(rows, w):
    projected = dot(rows, w, ((1,), (0,)))
    norm = lax.rsqrt(jnp.sum(projected * projected, axis=-1, keepdims=True) + 1e-06)
    return projected * norm, norm


class Loads:
    def __init__(self, sems):
        self.sems, self.used = sems, 0

    def start(self, source, target):
        copy = pltpu.make_async_copy(source, target, self.sems.at[self.used])
        self.used += 1
        copy.start()
        return copy


def load_weights(loads, tops, shards, w, side):
    copies = []
    for n, shard in enumerate(shards):
        top = pl.multiple_of(tops[n], 32)
        source = shard.at[:, pl.ds(side * WIDTH, WIDTH)]
        copies.append(loads.start(source, w.at[side, pl.ds(top, SHARE), :]))
    return copies


def load_rows(loads, pieces, raw):
    rows = pieces[0].shape[0]
    return [loads.start(p, raw.at[pl.ds(n * rows, rows), :]) for n, p in enumerate(pieces)]


def wait(*groups):
    for group in groups:
        for copy in group:
            copy.wait()


def meet(raw, w, mine, mult, offset):
    other = project(raw, w)[0].astype(jnp.bfloat16)
    logits = mult * dot(mine[...], other, ((1,), (1,))) + offset
    weight = (jax.nn.sigmoid(logits) * mult).astype(jnp.bfloat16)
    return dot(weight, other, ((1,), (0,)))


def own_kernel(mult_ref, offset_ref, tops, *refs):
    shards, (img, txt), (unit, norm, low, acc, w, raw, sems) = refs[:4], refs[4:6], refs[6:]
    mult, offset = mult_ref[0], offset_ref[0]
    loads = Loads(sems)
    ready = []
    for side, rows in enumerate((img, txt)):
        ready.append(
            load_weights(loads, tops, shards, w, side) + load_rows(loads, [rows], raw.at[side])
        )

    def step(side, carry):
        for n in range(2):
            pl.when(side == n)(functools.partial(wait, ready[n]))
        u, inv = project(raw[side], w[side])
        unit[side] = u
        norm[side] = inv
        low[side] = u.astype(jnp.bfloat16)
        return carry

    lax.fori_loop(0, 2, step, 0)
    logits = mult * dot(low[0], low[1], ((1,), (1,))) + offset
    line = lax.broadcasted_iota(jnp.int32, logits.shape, 0)
    column = lax.broadcasted_iota(jnp.int32, logits.shape, 1)
    sign = jnp.where(line == column, 1.0, -1.0)
    pair = (-sign * jax.nn.sigmoid(-sign * logits) * mult).astype(jnp.bfloat16)
    acc[0] = dot(pair, low[1], ((1,), (0,)))
    acc[1] = dot(pair, low[0], ((0,), (0,)))


def meet_kernel(mult_ref, offset_ref, tops, *refs):
    shards, (two_t, two_i), refs = refs[:4], refs[4:6], refs[6:]
    texts, images, refs = refs[:PIECES], refs[PIECES : 2 * PIECES], refs[2 * PIECES :]
    in_low, in_acc, acc, w, raw, low, sems = refs
    mult, offset = mult_ref[0], offset_ref[0]
    loads = Loads(sems)
    ready = []
    for side, two in enumerate((two_t, two_i)):
        ready.append(
            load_weights(loads, tops, shards, w, 1 - side)
            + load_rows(loads, [two], raw.at[side])
            + [loads.start(in_low.at[side], low.at[side])]
            + [loads.start(in_acc.at[side], acc.at[side])]
        )
    for side, ones in enumerate((texts, images)):
        ready.append(load_rows(loads, ones, raw.at[2 + side]))

    def step(turn, carry):
        for n in range(4):
            pl.when(turn == n)(functools.partial(wait, ready[n]))
        side = lax.rem(turn, 2)
        acc[side] += meet(raw[turn], w[1 - side], low.at[side], mult, offset)
        return carry

    lax.fori_loop(0, 4, step, 0)


def tail_kernel(mult_ref, offset_ref, tops, *refs):
    shards, refs = refs[:4], refs[4:]
    texts, images, refs = refs[:PIECES], refs[PIECES : 2 * PIECES], refs[2 * PIECES :]
    in_low, in_acc, in_unit, in_norm, in_x, tan, chunks, w, raw, low, acc, unit, norm, x, sems = refs
    mult, offset = mult_ref[0], offset_ref[0]
    loads = Loads(sems)
    ready = []
    for side, rows in enumerate((texts, images)):
        ready.append(
            load_weights(loads, tops, shards, w, 1 - side)
            + load_rows(loads, rows, raw.at[side])
            + [loads.start(in_low.at[side], low.at[side])]
            + [loads.start(in_acc.at[side], acc.at[side])]
        )
    last = [loads.start(in_unit, unit), loads.start(in_norm, norm), loads.start(in_x, x)]

    def step(side, carry):
        for n in range(2):
            pl.when(side == n)(functools.partial(wait, ready[n]))
        acc[side] += meet(raw[side], w[1 - side], low.at[side], mult, offset)
        return carry

    lax.fori_loop(0, 2, step, 0)
    wait(last)

    def finish(n, carry):
        rows = pl.ds(pl.multiple_of(n * 64, 64), 64)
        for side in range(2):
            u, a = unit[side, rows, :], acc[side, rows, :]
            along = jnp.sum(u * a, axis=-1, keepdims=True)
            tan[side, rows, :] = (norm[side, rows, :] * (a - u * along)).astype(jnp.bfloat16)
        return carry

    lax.fori_loop(0, ROWS // 64, finish, 0)
    fill(chunks, tan, x)


def fill(chunks, tan, x):
    def step(t, carry):
        for xh in range(2):
            g = dot(tan[t], x[t, xh], ((0,), (0,)))
            for block in range(4):
                top = block * SHARE
                pieces = [g[top + q * TALL : top + (q + 1) * TALL] for q in range(FOLD)]
                pieces.append(jnp.zeros((TALL, LANES - FOLD * SHARE), jnp.float32))
                chunks[t * 8 + block * 2 + xh] = jnp.concatenate(pieces, axis=1).astype(
                    jnp.bfloat16
                )
        return carry

    lax.fori_loop(0, 2, step, 0)


def keep_kernel(tan, x, chunks):
    fill(chunks, tan, x)


def weave_kernel(parts, order, out):
    for half in range(2):
        stack = []
        for block in range(4):
            for q in range(FOLD):
                stack.append(parts[half * 4 + block, :, q * SHARE : (q + 1) * SHARE])
        total = dot(jnp.concatenate(stack, axis=0), order[...], ((0,), (0,)))
        out[:, half * WIDTH : (half + 1) * WIDTH] = total.astype(jnp.bfloat16)


def call(kernel, outs, args, flops, scalars=0, scratch=(), anywhere=False):
    moved = sum(a.size * a.dtype.itemsize for a in (*args, *outs))
    spec = pl.BlockSpec(memory_space=pl.ANY) if anywhere else VMEM
    copies = (pltpu.SemaphoreType.DMA((24,)),) if anywhere else ()
    return pl.pallas_call(
        kernel,
        out_shape=outs,
        in_specs=[SMEM] * scalars + [spec] * (len(args) - scalars),
        out_specs=[VMEM] * len(outs),
        scratch_shapes=(*scratch, *copies),
        cost_estimate=pl.CostEstimate(flops=flops, bytes_accessed=moved, transcendentals=0),
        compiler_params=pltpu.CompilerParams(vmem_limit_bytes=56 * 1024 * 1024),
    )(*args)


def shaped(shape, dtype):
    return jax.ShapeDtypeStruct(shape, dtype)


def column_order():
    p = lax.iota(jnp.int32, WIDTH)
    y, xl = p // 576, p % 576 // 288
    q, z, i = p % 288 // 96, p % 96 // 12, p % 12
    natural = ((y * 8 + z) * 2 + xl) * COLS + q * 12 + i
    return (natural[:, None] == lax.iota(jnp.int32, WIDTH)[None, :]).astype(jnp.bfloat16)


def inner(
    picture_tower_inputs,
    caption_tower_inputs,
    halfwidth_parameter_matrix,
    affinity_multiplier,
    affinity_offset,
    precise_parameter_copy,
    gradient_mean_estimate,
    gradient_variance_estimate,
):
    bf16, f32 = jnp.bfloat16, jnp.float32
    img, txt = picture_tower_inputs, caption_tower_inputs
    order = column_order()
    w = halfwidth_parameter_matrix
    w = jnp.concatenate(
        [
            dot(w[:, :WIDTH], order, ((1,), (1,))).astype(bf16),
            dot(w[:, WIDTH:], order, ((1,), (1,))).astype(bf16),
        ],
        axis=1,
    )
    tops, shards = gather_weights(w)
    scalars = (affinity_multiplier, affinity_offset, tops)

    one_t, one_i, two_t, two_i, three_t, three_i = exchange(img, txt)
    c = lax.axis_index("c")

    def columns(rows, core):
        parts = rows.reshape(ROWS, 2, 2, SHARE)
        return jnp.where(core == 0, parts[:, :, 0], parts[:, :, 1]).transpose(1, 0, 2)

    give_x = jnp.stack([columns(img, 1 - c), columns(txt, 1 - c)])
    keep_x = jnp.stack([columns(img, c), columns(txt, c)])

    def both(shape, dtype):
        return shaped((2, *shape), dtype), pltpu.VMEM((2, *shape), dtype)

    mac = 2 * ROWS * WIDTH
    big, vbig = both((ROWS, WIDTH), f32)
    flat, vflat = both((ROWS, 1), f32)
    low, vlow = both((ROWS, WIDTH), bf16)
    vw = pltpu.VMEM((2, WIDTH, WIDTH), bf16)
    unit_of, norm_of, low_of, acc = call(
        own_kernel,
        (big, flat, low, big),
        (*scalars, *shards, img, txt),
        mac * (2 * WIDTH + 3 * ROWS),
        scalars=3,
        scratch=(vw, vlow),
        anywhere=True,
    )
    (acc,) = call(
        meet_kernel,
        (big,),
        (*scalars, *shards, two_t, two_i, *one_t, *one_i, low_of, acc),
        mac * (4 * WIDTH + 8 * ROWS),
        scalars=3,
        scratch=(vw, pltpu.VMEM((4, ROWS, WIDTH), bf16), vlow),
        anywhere=True,
    )
    chunk = shaped((16, TALL, LANES), bf16)
    tan, give = call(
        tail_kernel,
        (low, chunk),
        (*scalars, *shards, *three_t, *three_i, low_of, acc, unit_of, norm_of, give_x),
        mac * (3 * WIDTH + 4 * ROWS),
        scalars=3,
        scratch=(vw, vlow, vlow, vbig, vbig, vflat, pltpu.VMEM((2, 2, ROWS, SHARE), bf16)),
        anywhere=True,
    )
    got = swapped(give, "c")
    (keep,) = call(keep_kernel, (chunk,), (tan, keep_x), mac * WIDTH)
    img_tangent = dot(tan[0], order, ((1,), (0,))).astype(bf16)
    txt_tangent = dot(tan[1], order, ((1,), (0,))).astype(bf16)

    chip = (keep.astype(f32) + got.astype(f32)).astype(bf16)
    parts = lax.all_to_all(chip, ("y", "xl", "xh"), 0, 0, tiled=True)
    plane = jnp.sum(parts.astype(f32), axis=0).astype(bf16)
    parts = lax.all_to_all(plane.reshape(8, 12, LANES), "z", 0, 0, tiled=True)
    gradient = jnp.sum(parts.astype(f32), axis=0)[:, : FOLD * SHARE]
    gradient = gradient.reshape(12, FOLD, SHARE).transpose(2, 1, 0).reshape(SHARE, COLS)

    new_one = 0.9 * gradient_mean_estimate + 0.1 * gradient
    new_two = 0.95 * gradient_variance_estimate + 0.05 * gradient * gradient
    new_master = precise_parameter_copy - 0.001 * (
        new_one / (jnp.sqrt(new_two) + 1e-08) + 0.1 * precise_parameter_copy
    )
    mine = new_master.astype(bf16).reshape(SHARE, FOLD, 12).transpose(2, 1, 0)
    mine = jnp.pad(mine.reshape(1, 12, FOLD * SHARE), ((0, 0), (0, 0), (0, LANES - FOLD * SHARE)))
    line = lax.all_to_all(jnp.broadcast_to(mine, (8, 12, LANES)), "z", 0, 0, tiled=True)
    line = jnp.broadcast_to(line.reshape(1, TALL, LANES), (8, TALL, LANES))
    parts = lax.all_to_all(line, ("y", "xl"), 0, 0, tiled=True)
    (new_weights,) = call(
        weave_kernel, (shaped((SHARE, 2 * WIDTH), bf16),), (parts, order), 4 * SHARE * WIDTH * WIDTH
    )
    return (img_tangent, txt_tangent, new_master, new_one, new_two, new_weights)


def solution(mesh):
    fine = Mesh(mesh.devices.reshape(4, 8, 2, 2, 2), AXES)
    rows = P(DP + FSDP, None)
    state = P(FSDP, DP)
    return jax.shard_map(
        inner,
        mesh=fine,
        in_specs=(rows, rows, P(FSDP, None), P(), P(), state, state, state),
        out_specs=(rows, rows, state, state, state, P(FSDP, None)),
        check_vma=False,
    )
```

```python
import functools

import jax
import jax.numpy as jnp
from jax import lax
from jax.experimental import pallas as pl
from jax.experimental.pallas import tpu as pltpu
from jax.sharding import Mesh, PartitionSpec as P

PIECES = 2
LINE = ("y", "z")
AXES = ("y", "z", "xl", "xh", "c")
DP = ("y", "z", "xl")
FSDP = ("xh", "c")


def shifted(value, steps):
    count = lax.axis_size(LINE)
    return lax.ppermute(value, LINE, [(i, (i + steps) % count) for i in range(count)])


def swapped(value, axes):
    count = lax.axis_size(axes)
    return lax.ppermute(value, axes, [(i, count - 1 - i) for i in range(count)])


def gather_weights(raw, arrange):
    across = arrange(swapped(raw, ("xl", "xh")))
    own = arrange(raw)
    beside = swapped(own, "c")
    far = swapped(across, "c")
    xh, c = lax.axis_index("xh"), lax.axis_index("c")
    rows = raw.shape[0]
    tops = jnp.stack([2 * xh + c, 2 * xh + 1 - c, 2 - 2 * xh + c, 3 - 2 * xh - c]) * rows
    return tops.astype(jnp.int32), (own, beside, across, far)


def exchange(img, txt):
    even = lax.axis_index("xl") == 0
    two_t = shifted(txt, 1)
    two_i = shifted(img, -1)
    first = swapped(jnp.where(even, txt, img), "xl")
    one_t, one_i, three_t, three_i = [], [], [], []
    piece = txt.shape[0] // PIECES
    seconds = []
    for n in range(PIECES):
        cut = slice(n * piece, (n + 1) * piece)
        held = jnp.where(even, two_i[cut], two_t[cut])
        seconds.append(swapped(held, "xl"))
    for n in range(PIECES):
        cut = slice(n * piece, (n + 1) * piece)
        near, far = lax.optimization_barrier((first, seconds[n]))
        one_t.append(jnp.where(even, far, near[cut]))
        one_i.append(jnp.where(even, near[cut], far))
        three_t.append(shifted(one_t[n], 1))
        three_i.append(shifted(one_i[n], -1))
    return one_t, one_i, two_t, two_i, three_t, three_i


WIDTH = 1152
ROWS = 512
SHARE = 288
COLS = 36
FOLD = 3
TALL = SHARE // FOLD
LANES = 896
VMEM = pl.BlockSpec(memory_space=pltpu.VMEM)
SMEM = pl.BlockSpec(memory_space=pltpu.SMEM)


def dot(left, right, dims):
    return lax.dot_general(left, right, (dims, ((), ())), preferred_element_type=jnp.float32)


def project(rows, w):
    projected = dot(rows, w, ((1,), (0,)))
    norm = lax.rsqrt(jnp.sum(projected * projected, axis=-1, keepdims=True) + 1e-06)
    return projected * norm, norm


class Loads:
    def __init__(self, sems):
        self.sems, self.used = sems, 0

    def start(self, source, target):
        copy = pltpu.make_async_copy(source, target, self.sems.at[self.used])
        self.used += 1
        copy.start()
        return copy


def load_weights(loads, tops, shards, w, side):
    copies = []
    for n, shard in enumerate(shards):
        top = pl.multiple_of(tops[n], 32)
        source = shard.at[pl.ds(side * SHARE, SHARE), :]
        copies.append(loads.start(source, w.at[side, pl.ds(top, SHARE), :]))
    return copies


def load_rows(loads, pieces, raw):
    rows = pieces[0].shape[0]
    return [loads.start(p, raw.at[pl.ds(n * rows, rows), :]) for n, p in enumerate(pieces)]


def wait(*groups):
    for group in groups:
        for copy in group:
            copy.wait()


def meet(raw, w, mine, mult, offset):
    other = project(raw, w)[0].astype(jnp.bfloat16)
    logits = mult * dot(mine[...], other, ((1,), (1,))) + offset
    weight = (jax.nn.sigmoid(logits) * mult).astype(jnp.bfloat16)
    return dot(weight, other, ((1,), (0,)))


def own_kernel(mult_ref, offset_ref, tops, *refs):
    shards, (img, txt), (unit, norm, low, acc, w, raw, sems) = refs[:4], refs[4:6], refs[6:]
    mult, offset = mult_ref[0], offset_ref[0]
    loads = Loads(sems)
    ready = []
    for side, rows in enumerate((img, txt)):
        ready.append(
            load_weights(loads, tops, shards, w, side) + load_rows(loads, [rows], raw.at[side])
        )

    def step(side, carry):
        for n in range(2):
            pl.when(side == n)(functools.partial(wait, ready[n]))
        u, inv = project(raw[side], w[side])
        unit[side] = u
        norm[side] = inv
        low[side] = u.astype(jnp.bfloat16)
        return carry

    lax.fori_loop(0, 2, step, 0)
    logits = mult * dot(low[0], low[1], ((1,), (1,))) + offset
    line = lax.broadcasted_iota(jnp.int32, logits.shape, 0)
    column = lax.broadcasted_iota(jnp.int32, logits.shape, 1)
    sign = jnp.where(line == column, 1.0, -1.0)
    pair = (-sign * jax.nn.sigmoid(-sign * logits) * mult).astype(jnp.bfloat16)
    acc[0] = dot(pair, low[1], ((1,), (0,)))
    acc[1] = dot(pair, low[0], ((0,), (0,)))


def meet_kernel(mult_ref, offset_ref, tops, *refs):
    shards, (two_t, two_i), refs = refs[:4], refs[4:6], refs[6:]
    texts, images, refs = refs[:PIECES], refs[PIECES : 2 * PIECES], refs[2 * PIECES :]
    in_low, in_acc, acc, w, raw, low, sems = refs
    mult, offset = mult_ref[0], offset_ref[0]
    loads = Loads(sems)
    ready = []
    for side, two in enumerate((two_t, two_i)):
        ready.append(
            load_weights(loads, tops, shards, w, 1 - side)
            + load_rows(loads, [two], raw.at[side])
            + [loads.start(in_low.at[side], low.at[side])]
            + [loads.start(in_acc.at[side], acc.at[side])]
        )
    for side, ones in enumerate((texts, images)):
        ready.append(load_rows(loads, ones, raw.at[2 + side]))

    def step(turn, carry):
        for n in range(4):
            pl.when(turn == n)(functools.partial(wait, ready[n]))
        side = lax.rem(turn, 2)
        acc[side] += meet(raw[turn], w[1 - side], low.at[side], mult, offset)
        return carry

    lax.fori_loop(0, 4, step, 0)


def tail_kernel(mult_ref, offset_ref, tops, *refs):
    shards, refs = refs[:4], refs[4:]
    texts, images, refs = refs[:PIECES], refs[PIECES : 2 * PIECES], refs[2 * PIECES :]
    in_low, in_acc, in_unit, in_norm, in_x, tan, chunks, w, raw, low, acc, unit, norm, x, sems = refs
    mult, offset = mult_ref[0], offset_ref[0]
    loads = Loads(sems)
    ready = []
    for side, rows in enumerate((texts, images)):
        ready.append(
            load_weights(loads, tops, shards, w, 1 - side)
            + load_rows(loads, rows, raw.at[side])
            + [loads.start(in_low.at[side], low.at[side])]
            + [loads.start(in_acc.at[side], acc.at[side])]
        )
    last = [loads.start(in_unit, unit), loads.start(in_norm, norm), loads.start(in_x, x)]

    def step(side, carry):
        for n in range(2):
            pl.when(side == n)(functools.partial(wait, ready[n]))
        acc[side] += meet(raw[side], w[1 - side], low.at[side], mult, offset)
        return carry

    lax.fori_loop(0, 2, step, 0)
    wait(last)

    def finish(n, carry):
        rows = pl.ds(pl.multiple_of(n * 64, 64), 64)
        for side in range(2):
            u, a = unit[side, rows, :], acc[side, rows, :]
            along = jnp.sum(u * a, axis=-1, keepdims=True)
            tan[side, rows, :] = (norm[side, rows, :] * (a - u * along)).astype(jnp.bfloat16)
        return carry

    lax.fori_loop(0, ROWS // 64, finish, 0)
    fill(chunks, tan, x)


def fill(chunks, tan, x, ready=()):
    def step(turn, carry):
        for n, copies in enumerate(ready):
            pl.when(turn == 2 * n)(functools.partial(wait, copies))
        t, xh = turn // 2, lax.rem(turn, 2)
        g = dot(tan[t], x[t, xh], ((0,), (0,)))
        for block in range(4):
            top = block * SHARE
            pieces = [g[top + q * TALL : top + (q + 1) * TALL] for q in range(FOLD)]
            pieces.append(jnp.zeros((TALL, LANES - FOLD * SHARE), jnp.float32))
            whole = jnp.concatenate(pieces, axis=1).astype(jnp.bfloat16)
            chunks[t * 8 + block * 2 + xh] = whole
        return carry

    lax.fori_loop(0, 4, step, 0)


def keep_kernel(in_tan, in_i, in_t, chunks, tan, x, sems):
    loads = Loads(sems)
    ready = []
    for side, source in enumerate((in_i, in_t)):
        ready.append([loads.start(source, x.at[side]), loads.start(in_tan.at[side], tan.at[side])])
    fill(chunks, tan, x, ready)


def weave_kernel(parts, order, out):
    def step(n, carry):
        pieces = []
        for y in range(2):
            stack = []
            for block in range(2):
                for q in range(FOLD):
                    stack.append(parts[n * 4 + y * 2 + block, :, q * SHARE : (q + 1) * SHARE])
            pieces.append(dot(jnp.concatenate(stack, axis=0), order[...], ((0,), (0,))))
        lanes = pl.ds(pl.multiple_of(n * WIDTH, 128), WIDTH)
        out[:, lanes] = jnp.concatenate(pieces, axis=1).astype(jnp.bfloat16)
        return carry

    lax.fori_loop(0, 2, step, 0)


def call(kernel, outs, args, flops, scalars=0, scratch=(), anywhere=False, limit=56):
    moved = sum(a.size * a.dtype.itemsize for a in (*args, *outs))
    spec = pl.BlockSpec(memory_space=pl.ANY) if anywhere else VMEM
    copies = (pltpu.SemaphoreType.DMA((24,)),) if anywhere else ()
    return pl.pallas_call(
        kernel,
        out_shape=outs,
        in_specs=[SMEM] * scalars + [spec] * (len(args) - scalars),
        out_specs=[VMEM] * len(outs),
        scratch_shapes=(*scratch, *copies),
        cost_estimate=pl.CostEstimate(flops=flops, bytes_accessed=moved, transcendentals=0),
        compiler_params=pltpu.CompilerParams(vmem_limit_bytes=limit * 1024 * 1024),
    )(*args)


def shaped(shape, dtype):
    return jax.ShapeDtypeStruct(shape, dtype)


def column_order(width):
    p = lax.iota(jnp.int32, width)
    y, xl = p // 576, p % 576 // 288
    q, z, i = p % 288 // 96, p % 96 // 12, p % 12
    natural = ((y * 8 + z) * 2 + xl) * COLS + q * 12 + i
    return (natural[:, None] == lax.iota(jnp.int32, width)[None, :]).astype(jnp.bfloat16)


def inner(
    picture_tower_inputs,
    caption_tower_inputs,
    halfwidth_parameter_matrix,
    affinity_multiplier,
    affinity_offset,
    precise_parameter_copy,
    gradient_mean_estimate,
    gradient_variance_estimate,
):
    bf16, f32 = jnp.bfloat16, jnp.float32
    img, txt = picture_tower_inputs, caption_tower_inputs
    order = column_order(WIDTH)

    def arrange(w):
        sides = jnp.concatenate([w[:, :WIDTH], w[:, WIDTH:]], axis=0)
        return dot(sides, order, ((1,), (1,))).astype(bf16)

    tops, shards = gather_weights(halfwidth_parameter_matrix, arrange)
    scalars = (affinity_multiplier, affinity_offset, tops)
    one_t, one_i, two_t, two_i, three_t, three_i = exchange(img, txt)
    c = lax.axis_index("c")

    def columns(rows, core):
        parts = rows.reshape(ROWS, 2, 2, SHARE)
        return jnp.where(core == 0, parts[:, :, 0], parts[:, :, 1]).transpose(1, 0, 2)

    give_x = jnp.stack([columns(img, 1 - c), columns(txt, 1 - c)])
    keep_i, keep_t = columns(img, c), columns(txt, c)

    def both(shape, dtype):
        return shaped((2, *shape), dtype), pltpu.VMEM((2, *shape), dtype)

    mac = 2 * ROWS * WIDTH
    big, vbig = both((ROWS, WIDTH), f32)
    flat, vflat = both((ROWS, 1), f32)
    low, vlow = both((ROWS, WIDTH), bf16)
    vw = pltpu.VMEM((2, WIDTH, WIDTH), bf16)
    unit_of, norm_of, low_of, acc = call(
        own_kernel,
        (big, flat, low, big),
        (*scalars, *shards, img, txt),
        mac * (2 * WIDTH + 3 * ROWS),
        scalars=3,
        scratch=(vw, vlow),
        anywhere=True,
    )
    (acc,) = call(
        meet_kernel,
        (big,),
        (*scalars, *shards, two_t, two_i, *one_t, *one_i, low_of, acc),
        mac * (4 * WIDTH + 8 * ROWS),
        scalars=3,
        scratch=(vw, pltpu.VMEM((4, ROWS, WIDTH), bf16), vlow),
        anywhere=True,
    )
    chunk = shaped((16, TALL, LANES), bf16)
    tan, give = call(
        tail_kernel,
        (low, chunk),
        (*scalars, *shards, *three_t, *three_i, low_of, acc, unit_of, norm_of, give_x),
        mac * (3 * WIDTH + 4 * ROWS),
        scalars=3,
        scratch=(vw, vlow, vlow, vbig, vbig, vflat, pltpu.VMEM((2, 2, ROWS, SHARE), bf16)),
        anywhere=True,
    )
    got = swapped(give, "c")
    (keep,) = call(
        keep_kernel,
        (chunk,),
        (tan, keep_i, keep_t),
        mac * WIDTH,
        scratch=(vlow, pltpu.VMEM((2, 2, ROWS, SHARE), bf16)),
        anywhere=True,
    )
    img_tangent = dot(tan[0], order, ((1,), (0,))).astype(bf16)
    txt_tangent = dot(tan[1], order, ((1,), (0,))).astype(bf16)

    chip = (keep.astype(f32) + got.astype(f32)).astype(bf16)
    parts = lax.all_to_all(chip, ("y", "xl", "xh"), 0, 0, tiled=True)
    plane = jnp.sum(parts.astype(f32), axis=0).astype(bf16)
    parts = lax.all_to_all(plane.reshape(8, 12, LANES), "z", 0, 0, tiled=True)
    gradient = jnp.sum(parts.astype(f32), axis=0)[:, : FOLD * SHARE]
    gradient = gradient.reshape(12, FOLD, SHARE).transpose(2, 1, 0).reshape(SHARE, COLS)

    new_one = 0.9 * gradient_mean_estimate + 0.1 * gradient
    new_two = 0.95 * gradient_variance_estimate + 0.05 * gradient * gradient
    new_master = precise_parameter_copy - 0.001 * (
        new_one / (jnp.sqrt(new_two) + 1e-08) + 0.1 * precise_parameter_copy
    )
    mine = new_master.astype(bf16).reshape(SHARE, FOLD, 12).transpose(2, 1, 0)
    mine = jnp.pad(mine.reshape(1, 12, FOLD * SHARE), ((0, 0), (0, 0), (0, LANES - FOLD * SHARE)))
    line = lax.all_to_all(jnp.broadcast_to(mine, (8, 12, LANES)), "z", 0, 0, tiled=True)
    line = jnp.broadcast_to(line.reshape(1, TALL, LANES), (8, TALL, LANES))
    parts = lax.all_to_all(line, ("y", "xl"), 0, 0, tiled=True)
    (new_weights,) = call(
        weave_kernel,
        (shaped((SHARE, 2 * WIDTH), bf16),),
        (parts, column_order(WIDTH // 2)),
        2 * SHARE * WIDTH * WIDTH,
        limit=16,
    )
    return (img_tangent, txt_tangent, new_master, new_one, new_two, new_weights)


def solution(mesh):
    fine = Mesh(mesh.devices.reshape(4, 8, 2, 2, 2), AXES)
    rows = P(DP + FSDP, None)
    state = P(FSDP, DP)
    return jax.shard_map(
        inner,
        mesh=fine,
        in_specs=(rows, rows, P(FSDP, None), P(), P(), state, state, state),
        out_specs=(rows, rows, state, state, state, P(FSDP, None)),
        check_vma=False,
    )
```

```python
import jax
import jax.numpy as jnp
from jax import lax
from jax.experimental import pallas as pl
from jax.experimental.pallas import tpu as pltpu
from jax.sharding import Mesh, PartitionSpec as P

PIECES = 2
LINE = ("y", "z")
AXES = ("y", "z", "xl", "xh", "c")
DP = ("y", "z", "xl")
FSDP = ("xh", "c")


def shifted(value, steps):
    count = lax.axis_size(LINE)
    return lax.ppermute(value, LINE, [(i, (i + steps) % count) for i in range(count)])


def swapped(value, axes):
    count = lax.axis_size(axes)
    return lax.ppermute(value, axes, [(i, count - 1 - i) for i in range(count)])


def gather_weights(raw, arrange):
    across = arrange(swapped(raw, ("xl", "xh")))
    own = arrange(raw)
    beside = swapped(own, "c")
    far = swapped(across, "c")
    xh, c = lax.axis_index("xh"), lax.axis_index("c")
    rows = raw.shape[0]
    tops = jnp.stack([2 * xh + c, 2 * xh + 1 - c, 2 - 2 * xh + c, 3 - 2 * xh - c]) * rows
    return tops.astype(jnp.int32), (own, beside, across, far)


def exchange(img, txt):
    even = lax.axis_index("xl") == 0
    two_t = shifted(txt, 1)
    two_i = shifted(img, -1)
    first = swapped(jnp.where(even, txt, img), "xl")
    one_t, one_i, three_t, three_i = [], [], [], []
    piece = txt.shape[0] // PIECES
    seconds = []
    for n in range(PIECES):
        cut = slice(n * piece, (n + 1) * piece)
        held = jnp.where(even, two_i[cut], two_t[cut])
        seconds.append(swapped(held, "xl"))
    for n in range(PIECES):
        cut = slice(n * piece, (n + 1) * piece)
        near, far = lax.optimization_barrier((first, seconds[n]))
        one_t.append(jnp.where(even, far, near[cut]))
        one_i.append(jnp.where(even, near[cut], far))
        three_t.append(shifted(one_t[n], 1))
        three_i.append(shifted(one_i[n], -1))
    return one_t, one_i, two_t, two_i, three_t, three_i


WIDTH = 1152
ROWS = 512
SHARE = 288
COLS = 36
FOLD = 3
TALL = SHARE // FOLD
LANES = 896
VMEM = pl.BlockSpec(memory_space=pltpu.VMEM)
SMEM = pl.BlockSpec(memory_space=pltpu.SMEM)


def dot(left, right, dims):
    return lax.dot_general(left, right, (dims, ((), ())), preferred_element_type=jnp.float32)


def project(rows, w):
    projected = dot(rows, w, ((1,), (0,)))
    norm = lax.rsqrt(jnp.sum(projected * projected, axis=-1, keepdims=True) + 1e-06)
    return projected * norm, norm


class Loads:
    def __init__(self, sems):
        self.sems, self.used = sems, 0

    def plan(self, source, target):
        self.used += 1
        return pltpu.make_async_copy(source, target, self.sems.at[self.used - 1])


def start(*groups):
    for group in groups:
        for copy in group:
            copy.start()


def arrive(turn, ready, stride=1, extra=()):
    for n, copies in enumerate(ready):

        def land(n=n, copies=copies):
            wait(copies)
            if n == 0:
                start(*ready[1:], *extra)

        pl.when(turn == n * stride)(land)


def load_weights(loads, tops, shards, w, side):
    copies = []
    for n, shard in enumerate(shards):
        top = pl.multiple_of(tops[n], 32)
        source = shard.at[pl.ds(side * SHARE, SHARE), :]
        copies.append(loads.plan(source, w.at[side, pl.ds(top, SHARE), :]))
    return copies


def load_rows(loads, pieces, raw):
    rows = pieces[0].shape[0]
    return [loads.plan(p, raw.at[pl.ds(n * rows, rows), :]) for n, p in enumerate(pieces)]


def wait(*groups):
    for group in groups:
        for copy in group:
            copy.wait()


def meet(raw, w, mine, mult, offset):
    other = project(raw, w)[0].astype(jnp.bfloat16)
    logits = mult * dot(mine[...], other, ((1,), (1,))) + offset
    weight = (jax.nn.sigmoid(logits) * mult).astype(jnp.bfloat16)
    return dot(weight, other, ((1,), (0,)))


def own_kernel(mult_ref, offset_ref, tops, *refs):
    shards, (img, txt), (unit, norm, low, acc, w, raw, sems) = refs[:4], refs[4:6], refs[6:]
    mult, offset = mult_ref[0], offset_ref[0]
    loads = Loads(sems)
    ready = []
    for side, rows in enumerate((img, txt)):
        ready.append(
            load_weights(loads, tops, shards, w, side) + load_rows(loads, [rows], raw.at[side])
        )

    start(ready[0])

    def step(side, carry):
        arrive(side, ready)
        u, inv = project(raw[side], w[side])
        unit[side] = u
        norm[side] = inv
        low[side] = u.astype(jnp.bfloat16)
        return carry

    lax.fori_loop(0, 2, step, 0)
    logits = mult * dot(low[0], low[1], ((1,), (1,))) + offset
    line = lax.broadcasted_iota(jnp.int32, logits.shape, 0)
    column = lax.broadcasted_iota(jnp.int32, logits.shape, 1)
    sign = jnp.where(line == column, 1.0, -1.0)
    pair = (-sign * jax.nn.sigmoid(-sign * logits) * mult).astype(jnp.bfloat16)
    acc[0] = dot(pair, low[1], ((1,), (0,)))
    acc[1] = dot(pair, low[0], ((0,), (0,)))


def meet_kernel(mult_ref, offset_ref, tops, *refs):
    shards, (two_t, two_i), refs = refs[:4], refs[4:6], refs[6:]
    texts, images, refs = refs[:PIECES], refs[PIECES : 2 * PIECES], refs[2 * PIECES :]
    in_low, in_acc, acc, w, raw, low, sems = refs
    mult, offset = mult_ref[0], offset_ref[0]
    loads = Loads(sems)
    ready = []
    for side, two in enumerate((two_t, two_i)):
        ready.append(
            load_weights(loads, tops, shards, w, 1 - side)
            + load_rows(loads, [two], raw.at[side])
            + [loads.plan(in_low.at[side], low.at[side])]
            + [loads.plan(in_acc.at[side], acc.at[side])]
        )
    for side, ones in enumerate((texts, images)):
        ready.append(load_rows(loads, ones, raw.at[2 + side]))

    start(ready[0])

    def step(turn, carry):
        arrive(turn, ready)
        side = lax.rem(turn, 2)
        acc[side] += meet(raw[turn], w[1 - side], low.at[side], mult, offset)
        return carry

    lax.fori_loop(0, 4, step, 0)


def tail_kernel(mult_ref, offset_ref, tops, *refs):
    shards, refs = refs[:4], refs[4:]
    texts, images, refs = refs[:PIECES], refs[PIECES : 2 * PIECES], refs[2 * PIECES :]
    in_low, in_acc, in_unit, in_norm, *in_x = refs[:8]
    tan, chunks, w, raw, low, acc, unit, norm, x, sems = refs[8:]
    mult, offset = mult_ref[0], offset_ref[0]
    loads = Loads(sems)
    ready = []
    for side, rows in enumerate((texts, images)):
        ready.append(
            load_weights(loads, tops, shards, w, 1 - side)
            + load_rows(loads, rows, raw.at[side])
            + [loads.plan(in_low.at[side], low.at[side])]
            + [loads.plan(in_acc.at[side], acc.at[side])]
        )
    last = [loads.plan(in_unit, unit), loads.plan(in_norm, norm)]
    last += [loads.plan(source, x.at[n // 2, n % 2]) for n, source in enumerate(in_x)]

    start(ready[0])

    def step(side, carry):
        arrive(side, ready, extra=(last,))
        acc[side] += meet(raw[side], w[1 - side], low.at[side], mult, offset)
        return carry

    lax.fori_loop(0, 2, step, 0)
    wait(last)

    def finish(n, carry):
        rows = pl.ds(pl.multiple_of(n * 64, 64), 64)
        for side in range(2):
            u, a = unit[side, rows, :], acc[side, rows, :]
            along = jnp.sum(u * a, axis=-1, keepdims=True)
            tan[side, rows, :] = (norm[side, rows, :] * (a - u * along)).astype(jnp.bfloat16)
        return carry

    lax.fori_loop(0, ROWS // 64, finish, 0)
    fill(chunks, tan, x)


def fill(chunks, tan, x, ready=()):
    def step(turn, carry):
        arrive(turn, ready, stride=2)
        t, xh = turn // 2, lax.rem(turn, 2)
        g = dot(tan[t], x[t, xh], ((0,), (0,)))
        for block in range(4):
            top = block * SHARE
            pieces = [g[top + q * TALL : top + (q + 1) * TALL] for q in range(FOLD)]
            pieces.append(jnp.zeros((TALL, LANES - FOLD * SHARE), jnp.float32))
            whole = jnp.concatenate(pieces, axis=1).astype(jnp.bfloat16)
            chunks[t * 8 + block * 2 + xh] = whole
        return carry

    lax.fori_loop(0, 4, step, 0)


def keep_kernel(in_tan, *refs):
    in_x, (chunks, tan, x, sems) = refs[:4], refs[4:]
    loads = Loads(sems)
    ready = []
    for t in range(2):
        ready.append([loads.plan(in_tan.at[t], tan.at[t])])
        ready[t] += [loads.plan(in_x[2 * t + xh], x.at[t, xh]) for xh in range(2)]
    start(ready[0])
    fill(chunks, tan, x, ready)


def weave_kernel(parts, order, out):
    def step(n, carry):
        pieces = []
        for y in range(2):
            stack = []
            for block in range(2):
                for q in range(FOLD):
                    stack.append(parts[n * 4 + y * 2 + block, :, q * SHARE : (q + 1) * SHARE])
            pieces.append(dot(jnp.concatenate(stack, axis=0), order[...], ((0,), (0,))))
        lanes = pl.ds(pl.multiple_of(n * WIDTH, 128), WIDTH)
        out[:, lanes] = jnp.concatenate(pieces, axis=1).astype(jnp.bfloat16)
        return carry

    lax.fori_loop(0, 2, step, 0)


def call(kernel, outs, args, flops, scalars=0, scratch=(), anywhere=False, limit=56):
    moved = sum(a.size * a.dtype.itemsize for a in (*args, *outs))
    spec = pl.BlockSpec(memory_space=pl.ANY) if anywhere else VMEM
    copies = (pltpu.SemaphoreType.DMA((24,)),) if anywhere else ()
    return pl.pallas_call(
        kernel,
        out_shape=outs,
        in_specs=[SMEM] * scalars + [spec] * (len(args) - scalars),
        out_specs=[VMEM] * len(outs),
        scratch_shapes=(*scratch, *copies),
        cost_estimate=pl.CostEstimate(flops=flops, bytes_accessed=moved, transcendentals=0),
        compiler_params=pltpu.CompilerParams(vmem_limit_bytes=limit * 1024 * 1024),
    )(*args)


def shaped(shape, dtype):
    return jax.ShapeDtypeStruct(shape, dtype)


def column_order(width):
    p = lax.iota(jnp.int32, width)
    y, xl = p // 576, p % 576 // 288
    q, z, i = p % 288 // 96, p % 96 // 12, p % 12
    natural = ((y * 8 + z) * 2 + xl) * COLS + q * 12 + i
    return (natural[:, None] == lax.iota(jnp.int32, width)[None, :]).astype(jnp.bfloat16)


def inner(
    picture_tower_inputs,
    caption_tower_inputs,
    halfwidth_parameter_matrix,
    affinity_multiplier,
    affinity_offset,
    precise_parameter_copy,
    gradient_mean_estimate,
    gradient_variance_estimate,
):
    bf16, f32 = jnp.bfloat16, jnp.float32
    img, txt = picture_tower_inputs, caption_tower_inputs
    order = column_order(WIDTH)

    def arrange(w):
        sides = jnp.concatenate([w[:, :WIDTH], w[:, WIDTH:]], axis=0)
        return dot(sides, order, ((1,), (1,))).astype(bf16)

    tops, shards = gather_weights(halfwidth_parameter_matrix, arrange)
    scalars = (affinity_multiplier, affinity_offset, tops)
    one_t, one_i, two_t, two_i, three_t, three_i = exchange(img, txt)
    c = lax.axis_index("c")

    def columns(rows, core):
        cuts = [rows[:, n * SHARE : (n + 1) * SHARE] for n in range(4)]
        return [jnp.where(core == 0, cuts[2 * xh], cuts[2 * xh + 1]) for xh in range(2)]

    give_x = columns(img, 1 - c) + columns(txt, 1 - c)
    keep_x = columns(img, c) + columns(txt, c)

    def both(shape, dtype):
        return shaped((2, *shape), dtype), pltpu.VMEM((2, *shape), dtype)

    mac = 2 * ROWS * WIDTH
    big, vbig = both((ROWS, WIDTH), f32)
    flat, vflat = both((ROWS, 1), f32)
    low, vlow = both((ROWS, WIDTH), bf16)
    vw = pltpu.VMEM((2, WIDTH, WIDTH), bf16)
    unit_of, norm_of, low_of, acc = call(
        own_kernel,
        (big, flat, low, big),
        (*scalars, *shards, img, txt),
        mac * (2 * WIDTH + 3 * ROWS),
        scalars=3,
        scratch=(vw, vlow),
        anywhere=True,
    )
    (acc,) = call(
        meet_kernel,
        (big,),
        (*scalars, *shards, two_t, two_i, *one_t, *one_i, low_of, acc),
        mac * (4 * WIDTH + 8 * ROWS),
        scalars=3,
        scratch=(vw, pltpu.VMEM((4, ROWS, WIDTH), bf16), vlow),
        anywhere=True,
    )
    chunk = shaped((16, TALL, LANES), bf16)
    tan, give = call(
        tail_kernel,
        (low, chunk),
        (*scalars, *shards, *three_t, *three_i, low_of, acc, unit_of, norm_of, *give_x),
        mac * (3 * WIDTH + 4 * ROWS),
        scalars=3,
        scratch=(vw, vlow, vlow, vbig, vbig, vflat, pltpu.VMEM((2, 2, ROWS, SHARE), bf16)),
        anywhere=True,
    )
    got = swapped(give, "c")
    (keep,) = call(
        keep_kernel,
        (chunk,),
        (tan, *keep_x),
        mac * WIDTH,
        scratch=(vlow, pltpu.VMEM((2, 2, ROWS, SHARE), bf16)),
        anywhere=True,
    )
    img_tangent = dot(tan[0], order, ((1,), (0,))).astype(bf16)
    txt_tangent = dot(tan[1], order, ((1,), (0,))).astype(bf16)

    chip = (keep.astype(f32) + got.astype(f32)).astype(bf16)
    parts = lax.all_to_all(chip, ("y", "xl", "xh"), 0, 0, tiled=True)
    plane = jnp.sum(parts.astype(f32), axis=0).astype(bf16)
    parts = lax.all_to_all(plane.reshape(8, 12, LANES), "z", 0, 0, tiled=True)
    gradient = jnp.sum(parts.astype(f32), axis=0)[:, : FOLD * SHARE]
    gradient = gradient.reshape(12, FOLD, SHARE).transpose(2, 1, 0).reshape(SHARE, COLS)

    new_one = 0.9 * gradient_mean_estimate + 0.1 * gradient
    new_two = 0.95 * gradient_variance_estimate + 0.05 * gradient * gradient
    new_master = precise_parameter_copy - 0.001 * (
        new_one / (jnp.sqrt(new_two) + 1e-08) + 0.1 * precise_parameter_copy
    )
    mine = new_master.astype(bf16).reshape(SHARE, FOLD, 12).transpose(2, 1, 0)
    mine = jnp.pad(mine.reshape(1, 12, FOLD * SHARE), ((0, 0), (0, 0), (0, LANES - FOLD * SHARE)))
    line = lax.all_to_all(jnp.broadcast_to(mine, (8, 12, LANES)), "z", 0, 0, tiled=True)
    line = jnp.broadcast_to(line.reshape(1, TALL, LANES), (8, TALL, LANES))
    parts = lax.all_to_all(line, ("y", "xl"), 0, 0, tiled=True)
    (new_weights,) = call(
        weave_kernel,
        (shaped((SHARE, 2 * WIDTH), bf16),),
        (parts, column_order(WIDTH // 2)),
        2 * SHARE * WIDTH * WIDTH,
        limit=16,
    )
    return (img_tangent, txt_tangent, new_master, new_one, new_two, new_weights)


def solution(mesh):
    fine = Mesh(mesh.devices.reshape(4, 8, 2, 2, 2), AXES)
    rows = P(DP + FSDP, None)
    state = P(FSDP, DP)
    return jax.shard_map(
        inner,
        mesh=fine,
        in_specs=(rows, rows, P(FSDP, None), P(), P(), state, state, state),
        out_specs=(rows, rows, state, state, state, P(FSDP, None)),
        check_vma=False,
    )
```

```python
import jax
import jax.numpy as jnp
from jax import lax
from jax.experimental import pallas as pl
from jax.experimental.pallas import tpu as pltpu
from jax.sharding import Mesh, PartitionSpec as P

PIECES = 2
LINE = ("y", "z")
AXES = ("y", "z", "xl", "xh", "c")
DP = ("y", "z", "xl")
FSDP = ("xh", "c")


def shifted(value, steps):
    count = lax.axis_size(LINE)
    return lax.ppermute(value, LINE, [(i, (i + steps) % count) for i in range(count)])


def swapped(value, axes):
    count = lax.axis_size(axes)
    return lax.ppermute(value, axes, [(i, count - 1 - i) for i in range(count)])


def gather_weights(raw, arrange):
    across = arrange(swapped(raw, ("xl", "xh")))
    own = arrange(raw)
    beside = swapped(own, "c")
    far = swapped(across, "c")
    xh, c = lax.axis_index("xh"), lax.axis_index("c")
    rows = raw.shape[0]
    tops = jnp.stack([2 * xh + c, 2 * xh + 1 - c, 2 - 2 * xh + c, 3 - 2 * xh - c]) * rows
    return tops.astype(jnp.int32), (own, beside, across, far)


def exchange(img, txt):
    even = lax.axis_index("xl") == 0
    piece = txt.shape[0] // PIECES
    cuts = [slice(n * piece, (n + 1) * piece) for n in range(PIECES)]
    first = swapped(jnp.where(even, txt, img), "xl")
    two_t = [shifted(txt[cut], 1) for cut in cuts]
    two_i = [shifted(img[cut], -1) for cut in cuts]
    one_t, one_i, three_t, three_i, seconds = [], [], [], [], []
    for n in range(PIECES):
        at_t, at_i = lax.optimization_barrier((two_t[n], two_i[n]))
        held = jnp.where(even, at_i, at_t)
        seconds.append(swapped(held, "xl"))
    for n, cut in enumerate(cuts):
        near, far = lax.optimization_barrier((first, seconds[n]))
        one_t.append(jnp.where(even, far, near[cut]))
        one_i.append(jnp.where(even, near[cut], far))
        three_t.append(shifted(one_t[n], 1))
        three_i.append(shifted(one_i[n], -1))
    return one_t, one_i, two_t, two_i, three_t, three_i


WIDTH = 1152
ROWS = 512
SHARE = 288
COLS = 36
FOLD = 3
TALL = SHARE // FOLD
LANES = 896
VMEM = pl.BlockSpec(memory_space=pltpu.VMEM)
SMEM = pl.BlockSpec(memory_space=pltpu.SMEM)


def dot(left, right, dims):
    return lax.dot_general(left, right, (dims, ((), ())), preferred_element_type=jnp.float32)


def project(rows, w):
    projected = dot(rows, w, ((1,), (0,)))
    norm = lax.rsqrt(jnp.sum(projected * projected, axis=-1, keepdims=True) + 1e-06)
    return projected * norm, norm


class Loads:
    def __init__(self, sems):
        self.sems, self.used = sems, 0

    def plan(self, source, target):
        self.used += 1
        return pltpu.make_async_copy(source, target, self.sems.at[self.used - 1])


def start(*groups):
    for group in groups:
        for copy in group:
            copy.start()


def arrive(turn, ready, stride=1, extra=()):
    for n, copies in enumerate(ready):

        def land(n=n, copies=copies):
            wait(copies)
            if n == 0:
                start(*ready[1:], *extra)

        pl.when(turn == n * stride)(land)


def load_weights(loads, tops, shards, w, side):
    copies = []
    for n, shard in enumerate(shards):
        top = pl.multiple_of(tops[n], 32)
        source = shard.at[pl.ds(side * SHARE, SHARE), :]
        copies.append(loads.plan(source, w.at[side, pl.ds(top, SHARE), :]))
    return copies


def load_rows(loads, pieces, raw):
    rows = pieces[0].shape[0]
    return [loads.plan(p, raw.at[pl.ds(n * rows, rows), :]) for n, p in enumerate(pieces)]


def wait(*groups):
    for group in groups:
        for copy in group:
            copy.wait()


def meet(raw, w, mine, mult, offset):
    other = project(raw, w)[0].astype(jnp.bfloat16)
    logits = mult * dot(mine[...], other, ((1,), (1,))) + offset
    weight = (jax.nn.sigmoid(logits) * mult).astype(jnp.bfloat16)
    return dot(weight, other, ((1,), (0,)))


def own_kernel(mult_ref, offset_ref, tops, *refs):
    shards, (img, txt), (unit, norm, low, acc, w, raw, sems) = refs[:4], refs[4:6], refs[6:]
    mult, offset = mult_ref[0], offset_ref[0]
    loads = Loads(sems)
    ready = []
    for side, rows in enumerate((img, txt)):
        ready.append(
            load_weights(loads, tops, shards, w, side) + load_rows(loads, [rows], raw.at[side])
        )

    start(ready[0])

    def step(side, carry):
        arrive(side, ready)
        u, inv = project(raw[side], w[side])
        unit[side] = u
        norm[side] = inv
        low[side] = u.astype(jnp.bfloat16)
        return carry

    lax.fori_loop(0, 2, step, 0)
    logits = mult * dot(low[0], low[1], ((1,), (1,))) + offset
    line = lax.broadcasted_iota(jnp.int32, logits.shape, 0)
    column = lax.broadcasted_iota(jnp.int32, logits.shape, 1)
    sign = jnp.where(line == column, 1.0, -1.0)
    pair = (-sign * jax.nn.sigmoid(-sign * logits) * mult).astype(jnp.bfloat16)
    acc[0] = dot(pair, low[1], ((1,), (0,)))
    acc[1] = dot(pair, low[0], ((0,), (0,)))


def meet_kernel(mult_ref, offset_ref, tops, *refs):
    shards, refs = refs[:4], refs[4:]
    two_t, two_i, texts, images = (refs[n * PIECES : (n + 1) * PIECES] for n in range(4))
    in_low, in_acc, acc, w, raw, low, sems = refs[4 * PIECES :]
    mult, offset = mult_ref[0], offset_ref[0]
    loads = Loads(sems)
    ready = []
    for side, two in enumerate((two_t, two_i)):
        ready.append(
            load_weights(loads, tops, shards, w, 1 - side)
            + load_rows(loads, two, raw.at[side])
            + [loads.plan(in_low.at[side], low.at[side])]
            + [loads.plan(in_acc.at[side], acc.at[side])]
        )
    for side, ones in enumerate((texts, images)):
        ready.append(load_rows(loads, ones, raw.at[2 + side]))

    start(ready[0])

    def step(turn, carry):
        arrive(turn, ready)
        side = lax.rem(turn, 2)
        acc[side] += meet(raw[turn], w[1 - side], low.at[side], mult, offset)
        return carry

    lax.fori_loop(0, 4, step, 0)


def tail_kernel(mult_ref, offset_ref, tops, *refs):
    shards, refs = refs[:4], refs[4:]
    texts, images, refs = refs[:PIECES], refs[PIECES : 2 * PIECES], refs[2 * PIECES :]
    in_low, in_acc, in_unit, in_norm, *in_x = refs[:8]
    tan, chunks, w, raw, low, acc, unit, norm, x, sems = refs[8:]
    mult, offset = mult_ref[0], offset_ref[0]
    loads = Loads(sems)
    ready = []
    for side, rows in enumerate((texts, images)):
        ready.append(
            load_weights(loads, tops, shards, w, 1 - side)
            + load_rows(loads, rows, raw.at[side])
            + [loads.plan(in_low.at[side], low.at[side])]
            + [loads.plan(in_acc.at[side], acc.at[side])]
        )
    last = [loads.plan(in_unit, unit), loads.plan(in_norm, norm)]
    last += [loads.plan(source, x.at[n // 2, n % 2]) for n, source in enumerate(in_x)]

    start(ready[0])

    def step(side, carry):
        arrive(side, ready, extra=(last,))
        acc[side] += meet(raw[side], w[1 - side], low.at[side], mult, offset)
        return carry

    lax.fori_loop(0, 2, step, 0)
    wait(last)

    def finish(n, carry):
        rows = pl.ds(pl.multiple_of(n * 64, 64), 64)
        for side in range(2):
            u, a = unit[side, rows, :], acc[side, rows, :]
            along = jnp.sum(u * a, axis=-1, keepdims=True)
            tan[side, rows, :] = (norm[side, rows, :] * (a - u * along)).astype(jnp.bfloat16)
        return carry

    lax.fori_loop(0, ROWS // 64, finish, 0)
    fill(chunks, tan, x)


def fill(chunks, tan, x, ready=()):
    def step(turn, carry):
        arrive(turn, ready, stride=2)
        t, xh = turn // 2, lax.rem(turn, 2)
        g = dot(tan[t], x[t, xh], ((0,), (0,)))
        for block in range(4):
            top = block * SHARE
            pieces = [g[top + q * TALL : top + (q + 1) * TALL] for q in range(FOLD)]
            pieces.append(jnp.zeros((TALL, LANES - FOLD * SHARE), jnp.float32))
            whole = jnp.concatenate(pieces, axis=1).astype(jnp.bfloat16)
            chunks[t * 8 + block * 2 + xh] = whole
        return carry

    lax.fori_loop(0, 4, step, 0)


def keep_kernel(in_tan, *refs):
    in_x, (chunks, tan, x, sems) = refs[:4], refs[4:]
    loads = Loads(sems)
    ready = []
    for t in range(2):
        ready.append([loads.plan(in_tan.at[t], tan.at[t])])
        ready[t] += [loads.plan(in_x[2 * t + xh], x.at[t, xh]) for xh in range(2)]
    start(ready[0])
    fill(chunks, tan, x, ready)


def weave_kernel(parts, order, out):
    def step(n, carry):
        pieces = []
        for y in range(2):
            stack = []
            for block in range(2):
                for q in range(FOLD):
                    stack.append(parts[n * 4 + y * 2 + block, :, q * SHARE : (q + 1) * SHARE])
            pieces.append(dot(jnp.concatenate(stack, axis=0), order[...], ((0,), (0,))))
        lanes = pl.ds(pl.multiple_of(n * WIDTH, 128), WIDTH)
        out[:, lanes] = jnp.concatenate(pieces, axis=1).astype(jnp.bfloat16)
        return carry

    lax.fori_loop(0, 2, step, 0)


def call(kernel, outs, args, flops, scalars=0, scratch=(), anywhere=False, limit=56):
    moved = sum(a.size * a.dtype.itemsize for a in (*args, *outs))
    spec = pl.BlockSpec(memory_space=pl.ANY) if anywhere else VMEM
    copies = (pltpu.SemaphoreType.DMA((24,)),) if anywhere else ()
    return pl.pallas_call(
        kernel,
        out_shape=outs,
        in_specs=[SMEM] * scalars + [spec] * (len(args) - scalars),
        out_specs=[VMEM] * len(outs),
        scratch_shapes=(*scratch, *copies),
        cost_estimate=pl.CostEstimate(flops=flops, bytes_accessed=moved, transcendentals=0),
        compiler_params=pltpu.CompilerParams(vmem_limit_bytes=limit * 1024 * 1024),
    )(*args)


def shaped(shape, dtype):
    return jax.ShapeDtypeStruct(shape, dtype)


def column_order(width):
    p = lax.iota(jnp.int32, width)
    y, xl = p // 576, p % 576 // 288
    q, z, i = p % 288 // 96, p % 96 // 12, p % 12
    natural = ((y * 8 + z) * 2 + xl) * COLS + q * 12 + i
    return (natural[:, None] == lax.iota(jnp.int32, width)[None, :]).astype(jnp.bfloat16)


def inner(
    picture_tower_inputs,
    caption_tower_inputs,
    halfwidth_parameter_matrix,
    affinity_multiplier,
    affinity_offset,
    precise_parameter_copy,
    gradient_mean_estimate,
    gradient_variance_estimate,
):
    bf16, f32 = jnp.bfloat16, jnp.float32
    img, txt = picture_tower_inputs, caption_tower_inputs
    order = column_order(WIDTH)

    def arrange(w):
        sides = jnp.concatenate([w[:, :WIDTH], w[:, WIDTH:]], axis=0)
        return dot(sides, order, ((1,), (1,))).astype(bf16)

    tops, shards = gather_weights(halfwidth_parameter_matrix, arrange)
    scalars = (affinity_multiplier, affinity_offset, tops)
    one_t, one_i, two_t, two_i, three_t, three_i = exchange(img, txt)
    c = lax.axis_index("c")

    def columns(rows, core):
        cuts = [rows[:, n * SHARE : (n + 1) * SHARE] for n in range(4)]
        return [jnp.where(core == 0, cuts[2 * xh], cuts[2 * xh + 1]) for xh in range(2)]

    give_x = columns(img, 1 - c) + columns(txt, 1 - c)
    keep_x = columns(img, c) + columns(txt, c)

    def both(shape, dtype):
        return shaped((2, *shape), dtype), pltpu.VMEM((2, *shape), dtype)

    mac = 2 * ROWS * WIDTH
    big, vbig = both((ROWS, WIDTH), f32)
    flat, vflat = both((ROWS, 1), f32)
    low, vlow = both((ROWS, WIDTH), bf16)
    vw = pltpu.VMEM((2, WIDTH, WIDTH), bf16)
    unit_of, norm_of, low_of, acc = call(
        own_kernel,
        (big, flat, low, big),
        (*scalars, *shards, img, txt),
        mac * (2 * WIDTH + 3 * ROWS),
        scalars=3,
        scratch=(vw, vlow),
        anywhere=True,
    )
    (acc,) = call(
        meet_kernel,
        (big,),
        (*scalars, *shards, *two_t, *two_i, *one_t, *one_i, low_of, acc),
        mac * (4 * WIDTH + 8 * ROWS),
        scalars=3,
        scratch=(vw, pltpu.VMEM((4, ROWS, WIDTH), bf16), vlow),
        anywhere=True,
    )
    chunk = shaped((16, TALL, LANES), bf16)
    tan, give = call(
        tail_kernel,
        (low, chunk),
        (*scalars, *shards, *three_t, *three_i, low_of, acc, unit_of, norm_of, *give_x),
        mac * (3 * WIDTH + 4 * ROWS),
        scalars=3,
        scratch=(vw, vlow, vlow, vbig, vbig, vflat, pltpu.VMEM((2, 2, ROWS, SHARE), bf16)),
        anywhere=True,
    )
    got = swapped(give, "c")
    (keep,) = call(
        keep_kernel,
        (chunk,),
        (tan, *keep_x),
        mac * WIDTH,
        scratch=(vlow, pltpu.VMEM((2, 2, ROWS, SHARE), bf16)),
        anywhere=True,
    )
    img_tangent = dot(tan[0], order, ((1,), (0,))).astype(bf16)
    txt_tangent = dot(tan[1], order, ((1,), (0,))).astype(bf16)

    chip = (keep.astype(f32) + got.astype(f32)).astype(bf16)
    parts = lax.all_to_all(chip, ("y", "xl", "xh"), 0, 0, tiled=True)
    plane = jnp.sum(parts.astype(f32), axis=0).astype(bf16)
    parts = lax.all_to_all(plane.reshape(8, 12, LANES), "z", 0, 0, tiled=True)
    gradient = jnp.sum(parts.astype(f32), axis=0)[:, : FOLD * SHARE]
    gradient = gradient.reshape(12, FOLD, SHARE).transpose(2, 1, 0).reshape(SHARE, COLS)

    new_one = 0.9 * gradient_mean_estimate + 0.1 * gradient
    new_two = 0.95 * gradient_variance_estimate + 0.05 * gradient * gradient
    new_master = precise_parameter_copy - 0.001 * (
        new_one / (jnp.sqrt(new_two) + 1e-08) + 0.1 * precise_parameter_copy
    )
    mine = new_master.astype(bf16).reshape(SHARE, FOLD, 12).transpose(2, 1, 0)
    mine = jnp.pad(mine.reshape(1, 12, FOLD * SHARE), ((0, 0), (0, 0), (0, LANES - FOLD * SHARE)))
    line = lax.all_to_all(jnp.broadcast_to(mine, (8, 12, LANES)), "z", 0, 0, tiled=True)
    line = jnp.broadcast_to(line.reshape(1, TALL, LANES), (8, TALL, LANES))
    parts = lax.all_to_all(line, ("y", "xl"), 0, 0, tiled=True)
    (new_weights,) = call(
        weave_kernel,
        (shaped((SHARE, 2 * WIDTH), bf16),),
        (parts, column_order(WIDTH // 2)),
        2 * SHARE * WIDTH * WIDTH,
        limit=16,
    )
    return (img_tangent, txt_tangent, new_master, new_one, new_two, new_weights)


def solution(mesh):
    fine = Mesh(mesh.devices.reshape(4, 8, 2, 2, 2), AXES)
    rows = P(DP + FSDP, None)
    state = P(FSDP, DP)
    return jax.shard_map(
        inner,
        mesh=fine,
        in_specs=(rows, rows, P(FSDP, None), P(), P(), state, state, state),
        out_specs=(rows, rows, state, state, state, P(FSDP, None)),
        check_vma=False,
    )
```
